32 devices in a mesh: slab: 4 (over y, core), grp: 8 (over z, x).
Axes of the slice: x: 2, y: 2, z: 4, core: 2. Of those that a mesh axis runs over, the one named last changes fastest.
Arguments:
- diag_jac: bfloat16 [384, 625, 625], P(('slab', 'grp')), may hold values from -0.75 to 0.75
- xface_jac: bfloat16 [384, 2, 15625], P(('slab', 'grp')), may hold values from -1.5 to 1.5
- side_jac: bfloat16 [384, 4, 15625], P(('slab', 'grp')), may hold values from -1.5 to 1.5
- orient: int32 [384], P(('slab', 'grp')), may hold values from 0 to 3
- owner: int32 [384], P(('slab', 'grp')), may hold values from 0 to 1, as said below
Outputs:
- agglomerated: bfloat16 [2304, 7, 1600], P(('slab', 'grp'))
The draws below stay inside these ranges and needn't reach their ends.
Inputs may be any that keep to these rules, and one draw needn't show every extreme that they name: An element's owner is a grp index below 2 on its own slab. Among the 12 elements of one device at most 9 share an owner; on every slab one owner receives exactly 9 elements from every device of that slab.
All inputs are finite; a program needn't handle non-finite values.
Results may differ from the reference program's by a relative error of at most 0.001.
Values may be sent and summed in bfloat16 or wider, within the bound.
No kernel may reach another device: no remote copies, remote signals or barrier semaphores. Data moves between devices by JAX's collectives and lax.ppermute only.
A program may use at most 64 MiB of HBM per device.

```python
import jax
import jax.numpy as jnp
import numpy as np
from jax import lax

NV = 5
PF = 4
PM = 2
PC = 1
E_DEV = 12
NF = 625
NFACE = 125
NCOARSE = 40
MOST = 9
SLOTS = 72
ELEMS = 384
N_SLAB = 4
N_GRP = 8


def draw_owner(key, part):
    devices = N_SLAB * N_GRP
    owners_n = N_GRP // 4
    most = max(2, 3 * E_DEV // (2 * owners_n))
    full = jax.random.randint(jax.random.fold_in(key, 11), (N_SLAB,), 0, owners_n)
    full_dev = jnp.repeat(full, N_GRP)
    keys = jax.random.split(jax.random.fold_in(key, 12), devices)
    orders = jax.vmap(lambda single: jax.random.permutation(single, E_DEV))(keys)
    offsets = jax.random.randint(jax.random.fold_in(key, 13), (devices,), 0, owners_n - 1)
    places = jnp.arange(E_DEV, dtype=jnp.int32)[None, :]
    others = (full_dev[:, None] + 1 + (offsets[:, None] + places - most) % (owners_n - 1)) % owners_n
    values = jnp.where(places < most, full_dev[:, None], others)
    inverse = jnp.argsort(orders, axis=1)
    result = jnp.take_along_axis(values, inverse, axis=1)
    return result.reshape(-1).astype(jnp.int32)


def touch_ends(values, own_key, least, high):
    shape = values.shape
    index_at = [jax.random.randint(jax.random.fold_in(own_key, axis), (), 0, shape[axis]) for axis in range(len(shape))]
    values = values.at[tuple(index_at)].set(least)
    longest = shape.index(max(shape))
    index_at[longest] = (index_at[longest] + 1) % shape[longest]
    return values.at[tuple(index_at)].set(high)


def level_of(rng, shape, cuts, least, top_value):
    def one(position, shards_of):
        steps = jax.random.uniform(jax.random.fold_in(jax.random.fold_in(rng, 6), position), (shards_of,), jnp.float32, least / len(cuts), top_value / len(cuts))
        return jnp.repeat(jnp.exp(steps), shape[position] // shards_of).reshape((-1,) + (1,) * (len(shape) - position - 1))

    level = one(*cuts[0])
    for cut in cuts[1:]:
        level = level * one(*cut)
    return level


def scatter_about(rng, shape, deviation, reach, cuts=(), kind=jnp.bfloat16):
    values = jax.random.normal(rng, shape, jnp.float32) * deviation
    if len(cuts) > 0:
        values = level_of(rng, shape, cuts, -0.22, 0.18) * values
    return jnp.clip(values, min=-reach, max=reach).astype(kind)


def setup_inputs(seed: int = 0) -> dict:
    arg_keys = jax.random.split(jax.random.key(seed), 6)
    return {
        "diag_jac": scatter_about(arg_keys[0], (ELEMS, NF, NF), 0.125, 0.75, ((0, 32),)),
        "xface_jac": scatter_about(arg_keys[1], (ELEMS, 2, NFACE * NFACE), 0.25, 1.5, ((0, 32),)),
        "side_jac": scatter_about(arg_keys[2], (ELEMS, 4, NFACE * NFACE), 0.25, 1.5, ((0, 32),)),
        "orient": touch_ends(jax.random.randint(arg_keys[3], (ELEMS,), 0, 4), jax.random.fold_in(arg_keys[3], 1), 0, 3).astype(jnp.int32),
        "owner": draw_owner(jax.random.fold_in(arg_keys[5], 71), 0),
    }


def gll_points(degree):
    if degree == 1:
        return np.array([-1.0, 1.0])
    if degree == 2:
        return np.array([-1.0, 0.0, 1.0])
    if degree == 3:
        inner_pt = np.sqrt(0.2)
        return np.array([-1.0, -inner_pt, inner_pt, 1.0])
    inner_pt = np.sqrt(3.0 / 7.0)
    return np.array([-1.0, -inner_pt, 0.0, inner_pt, 1.0])

def lagrange(source_deg, target_deg):
    source = gll_points(source_deg)
    target = gll_points(target_deg)
    result = np.ones((target_deg + 1, source_deg + 1))
    for j in range(source_deg + 1):
        for m in range(source_deg + 1):
            if m != j:
                result[:, j] = result[:, j] * (target - source[m]) / (source[j] - source[m])
    return result

def grid_coords(nvars, side, dims):
    flat = np.arange(nvars * side ** dims)
    parts = []
    for power in range(dims, -1, -1):
        parts.append(flat // side ** power % (side if power < dims else nvars))
    return parts

def turn_table(nvars, side, with_x):
    if with_x:
        coords = grid_coords(nvars, side, 3)
        first, second = (coords[2], coords[3])
    else:
        coords = grid_coords(nvars, side, 2)
        first, second = (coords[1], coords[2])
    tables = []
    for turns in range(4):
        if with_x:
            index = ((coords[0] * side + coords[1]) * side + first) * side + second
        else:
            index = (coords[0] * side + first) * side + second
        tables.append(index)
        first, second = (side - 1 - second, first)
    return np.stack(tables).astype(np.int32)

def build_tables(nvars, fine_deg, mid_deg, coarse_deg):
    fine_mid = lagrange(mid_deg, fine_deg)
    mid_coarse = lagrange(coarse_deg, mid_deg)

    def cube(line):
        return np.kron(np.eye(nvars), np.kron(np.kron(line, line), line))
    upper = cube(fine_mid)
    lower = cube(mid_coarse)
    count = fine_deg + 1
    coords = grid_coords(nvars, count, 3)
    faces = []
    for axis_num in (1, 2, 3):
        for level in (0, fine_deg):
            faces.append(upper[coords[axis_num] == level])
    face_rows = np.stack(faces)
    coarse_turns = turn_table(nvars, coarse_deg + 1, True)
    face_turns = turn_table(nvars, count, False)
    return (upper.astype(np.float32), lower.astype(np.float32), face_rows.astype(np.float32), coarse_turns, face_turns)

def galerkin(blocks, left, right, lower):
    high = lax.Precision.HIGHEST
    inner = jnp.einsum('efab,fbm->efam', blocks.astype(jnp.float32), right, precision=high)
    middle = jnp.einsum('fan,efam->efnm', left, inner, precision=high)
    half = jnp.einsum('efnm,md->efnd', middle, lower, precision=high)
    return jnp.einsum('nc,efnd->efcd', lower, half, precision=high)

def reference(diag_jac, xface_jac, side_jac, orient, owner):
    upper, lower, face_rows, coarse_turns, face_turns = build_tables(NV, PF, PM, PC)
    upper = jnp.asarray(upper)
    lower = jnp.asarray(lower)
    face_rows = jnp.asarray(face_rows)
    coarse_turns = jnp.asarray(coarse_turns)
    devices = N_SLAB * N_GRP
    ncoarse = NCOARSE
    side_left = jnp.stack([face_rows[2], face_rows[3], face_rows[4], face_rows[5]])
    side_right = jnp.stack([face_rows[3], face_rows[2], face_rows[5], face_rows[4]])

    def per_device(items):
        diag, xface, side, turns = items
        xface = xface.reshape(E_DEV, 2, NFACE, NFACE)
        side = side.reshape(E_DEV, 4, NFACE, NFACE)
        perm = jnp.take(coarse_turns, turns, axis=0)
        diag_c = galerkin(diag[:, None], upper[None], upper[None], lower)[:, 0]
        plus_c = galerkin(xface[:, 0:1], face_rows[1:2], face_rows[0:1], lower)[:, 0]
        plus_c = jnp.take_along_axis(plus_c, perm[:, None, :], axis=2)
        sent = galerkin(xface[:, 1:2], face_rows[0:1], face_rows[1:2], lower)[:, 0]
        sent = jnp.take_along_axis(sent, perm[:, :, None], axis=1)
        side_c = galerkin(side, side_left, side_right, lower)
        return (diag_c, plus_c, sent, side_c)
    diag_c, plus_c, sent, side_c = lax.map(per_device, (diag_jac.reshape(devices, E_DEV, NF, NF), xface_jac.reshape(devices, E_DEV, 2, NFACE * NFACE), side_jac.reshape(devices, E_DEV, 4, NFACE * NFACE), orient.reshape(devices, E_DEV)))
    sent = sent.reshape(N_SLAB, N_GRP * E_DEV, ncoarse, ncoarse)
    minus_c = jnp.roll(sent, 1, axis=0).reshape(devices, E_DEV, ncoarse, ncoarse)
    rows = jnp.concatenate([diag_c[:, :, None], minus_c[:, :, None], plus_c[:, :, None], side_c], axis=2)
    rows = rows.astype(jnp.bfloat16).reshape(devices * E_DEV, 7, ncoarse * ncoarse)
    owners_dev = owner.reshape(devices, E_DEV)
    earlier = jnp.arange(E_DEV)[None, :] < jnp.arange(E_DEV)[:, None]
    same = owners_dev[:, :, None] == owners_dev[:, None, :]
    rank = lax.optimization_barrier(jnp.sum((same & earlier[None]).astype(jnp.int32), axis=2))
    device_ids = jnp.arange(devices, dtype=jnp.int32)
    slab_ids = (device_ids // N_GRP)[:, None]
    grp_ids = (device_ids % N_GRP)[:, None]
    flat = ((slab_ids * N_GRP + owners_dev) * SLOTS + grp_ids * MOST + rank).astype(jnp.int32)
    result = jnp.zeros((N_SLAB * N_GRP * SLOTS, 7, ncoarse * ncoarse), jnp.bfloat16)
    return result.at[flat.reshape(-1)].set(rows)
```

```python
import functools

import jax
import jax.numpy as jnp
import numpy as np
from jax import lax
from jax.experimental import pallas as pl
from jax.experimental.pallas import tpu as pltpu
from jax.sharding import PartitionSpec as P

NV = 5
PF = 4
PM = 2
PC = 1
LANES = 128
F32 = jnp.float32
BF16 = jnp.bfloat16


def gll_points(degree):
    if degree == 1:
        return np.array([-1.0, 1.0])
    if degree == 2:
        return np.array([-1.0, 0.0, 1.0])
    inner_pt = np.sqrt(3.0 / 7.0)
    return np.array([-1.0, -inner_pt, 0.0, inner_pt, 1.0])


def lagrange(source_deg, target_deg):
    source = gll_points(source_deg)
    target = gll_points(target_deg)
    result = np.ones((target_deg + 1, source_deg + 1))
    for j in range(source_deg + 1):
        for m in range(source_deg + 1):
            if m != j:
                result[:, j] = result[:, j] * (target - source[m]) / (source[j] - source[m])
    return result


def round_up(value, step):
    return -(-value // step) * step


def split(table):
    leading = table.astype(np.float32).astype(BF16)
    remainder = (table - leading.astype(np.float64)).astype(np.float32).astype(BF16)
    return leading, remainder


LINE = lagrange(PM, PF) @ lagrange(PC, PM)
SIDE = PC + 1
NCOARSE = NV * SIDE**3
NFACE = NV * (PF + 1) ** 2
PLANE = SIDE**2
UNIT = PLANE * NV * PLANE
FACE = NV * UNIT
VROW = SIDE**3 * NCOARSE
NFACES = 6
DIAG_AT = round_up(NFACES * FACE, LANES)
ROW_TILES = round_up(DIAG_AT + NCOARSE * NCOARSE, LANES) // LANES
LEFT_TILES = round_up(VROW, LANES) // LANES


def face_table():
    face = np.kron(LINE, LINE)
    table = np.kron(face, np.kron(np.eye(NV), face))
    leading, remainder = split(table)
    out = np.zeros((table.shape[0], 2 * LANES), BF16)
    out[:, :UNIT] = leading
    out[:, LANES : LANES + UNIT] = remainder
    return out


def diag_tables():
    table = np.kron(np.eye(NV), np.kron(np.kron(LINE, LINE), LINE))
    leading, remainder = split(table)
    right = np.zeros((table.shape[0], 2 * LANES), BF16)
    right[:, :NCOARSE] = leading
    right[:, LANES : LANES + NCOARSE] = remainder
    left = np.concatenate([leading.T, remainder.T], axis=0)
    return right, left


def plane_turns():
    flat = np.arange(PLANE)
    first, second = flat // SIDE, flat % SIDE
    tables = []
    for _ in range(4):
        tables.append(first * SIDE + second)
        first, second = SIDE - 1 - second, first
    return tables


def turn_tables():
    out = np.zeros((2, UNIT, 4 * LANES), BF16)
    for o, table in enumerate(plane_turns()):
        for c in range(PLANE):
            for w in range(NV):
                for d in range(PLANE):
                    new = (c * NV + w) * PLANE + d
                    out[0, (c * NV + w) * PLANE + table[d], o * LANES + new] = 1
                    out[1, (table[c] * NV + w) * PLANE + d, o * LANES + new] = 1
    return out


def spread_tables():
    half = VROW % LANES
    out = np.zeros((NFACES, UNIT, 2 * LEFT_TILES * LANES), BF16)

    def full(plane, axis, level):
        pair = [plane // SIDE, plane % SIDE]
        pair.insert(axis, level)
        return (pair[0] * SIDE + pair[1]) * SIDE + pair[2]

    for face in range(NFACES):
        axis, high = face // 2, face % 2
        for c in range(PLANE):
            for w in range(NV):
                for d in range(PLANE):
                    row = full(c, axis, high)
                    col = w * SIDE**3 + full(d, axis, 1 - high)
                    unit = (c * NV + w) * PLANE + d
                    out[face, unit, row * NCOARSE + col] = 1
                    out[face, unit, LEFT_TILES * LANES + half + row * NCOARSE + col] = 1
    return out


def face_kernel(x_ref, table_ref, out_ref, scratch, *, rows):
    width = table_ref.shape[0]
    parts = [x_ref[:, v * width : (v + 1) * width] for v in range(NV)]
    y = jnp.dot(jnp.concatenate(parts, axis=0), table_ref[...], preferred_element_type=F32)
    y = y[:, :LANES] + y[:, LANES:]
    for v in range(NV):
        scratch[:, v * UNIT : (v + 1) * UNIT] = y[v * rows : (v + 1) * rows, :UNIT]
    out_ref[...] = scratch[...].astype(BF16)


def xface_kernel(x_ref, table_ref, turn_ref, orient_ref, plus_ref, sent_ref, scratch, *, elems):
    width = table_ref.shape[0]
    rows = 2 * elems
    parts = [x_ref[:, v * width : (v + 1) * width] for v in range(NV)]
    y = jnp.dot(jnp.concatenate(parts, axis=0), table_ref[...], preferred_element_type=F32)
    y = (y[:, :LANES] + y[:, LANES:])[:, :UNIT].astype(BF16)
    for which, out_ref in enumerate((plus_ref, sent_ref)):
        start = which * elems
        mine = jnp.concatenate([y[v * rows + start : v * rows + start + elems] for v in range(NV)], axis=0)
        turned = jnp.dot(mine, turn_ref[which], preferred_element_type=F32)
        for v in range(NV):
            piece = turned[v * elems : (v + 1) * elems]
            total = jnp.zeros((elems, LANES), F32)
            for o in range(4):
                total = jnp.where(orient_ref[...] == o, piece[:, o * LANES : (o + 1) * LANES], total)
            scratch[:, v * UNIT : (v + 1) * UNIT] = total[:, :UNIT]
        out_ref[...] = scratch[...].astype(BF16)


def diag_kernel(block_ref, right_ref, left_ref, out_ref, coarse, flat, *, elems):
    e = pl.program_id(0)
    y = jnp.dot(block_ref[...], right_ref[...], preferred_element_type=F32)
    z = y[:, :LANES] + y[:, LANES:]
    high = z.astype(BF16)
    low = (z - high.astype(F32)).astype(BF16)
    g = jnp.dot(left_ref[...], jnp.concatenate([high, low], axis=1), preferred_element_type=F32)
    g = g[:NCOARSE, :LANES] + g[NCOARSE:, :LANES] + g[:NCOARSE, LANES:]
    coarse[pl.ds(e * NCOARSE, NCOARSE), :] = g

    @pl.when(e == elems - 1)
    def _():
        flat[...] = jnp.zeros_like(flat)
        for c in range(NCOARSE):
            piece = coarse[pl.ds(c, elems, stride=NCOARSE), :]
            flat[:elems, c * NCOARSE : (c + 1) * NCOARSE] = piece[:, :NCOARSE]
        out_ref[...] = flat[...].astype(BF16)


def pack_kernel(minus_ref, plus_ref, side_ref, diag_ref, placer_ref, out_ref, rows_scr, out_scr, *, elems):
    rows_scr[...] = jnp.zeros_like(rows_scr)
    rows_scr[:, :FACE] = minus_ref[...].astype(F32)
    rows_scr[:, FACE : 2 * FACE] = plus_ref[...].astype(F32)
    for f in range(NFACES - 2):
        start = (2 + f) * FACE
        rows_scr[:, start : start + FACE] = side_ref[f * elems : (f + 1) * elems].astype(F32)
    rows_scr[:, DIAG_AT : DIAG_AT + diag_ref.shape[1]] = diag_ref[...].astype(F32)
    slots = placer_ref.shape[0]
    packed = jnp.dot(placer_ref[...], rows_scr[...].astype(BF16), preferred_element_type=F32)
    for j in range(ROW_TILES):
        out_scr[pl.ds(j, slots, stride=ROW_TILES), :] = packed[:, j * LANES : (j + 1) * LANES]
    out_ref[...] = out_scr[...].astype(BF16).reshape(out_ref.shape)


def unpack_kernel(where_ref, *refs, owners_n, most):
    n_src = len(refs) - 5
    sources, spread_ref, out_ref, tiles, flat, full = (
        refs[:n_src], refs[n_src], refs[n_src + 1], refs[n_src + 2], refs[n_src + 3], refs[n_src + 4],
    )
    slots = out_ref.shape[0]
    me = where_ref[0]

    @pl.when(me >= owners_n)
    def _():
        out_ref[...] = jnp.zeros_like(out_ref)

    @pl.when(me < owners_n)
    def _():
        step = most * ROW_TILES
        for a in range(n_src):
            for o in range(owners_n):
                chunk = lax.rem(me - o + owners_n, owners_n)
                value = sources[a][chunk].astype(F32).reshape(step, LANES)
                tiles[pl.ds((a * owners_n + o) * step, step), :] = value
        for j in range(ROW_TILES):
            flat[:, j * LANES : (j + 1) * LANES] = tiles[pl.ds(j, slots, stride=ROW_TILES), :]
        even = list(range(0, NV, 2))
        odd = list(range(1, NV, 2))
        half = LEFT_TILES * LANES
        for f in range(NFACES):
            def units(vs):
                cuts = [f * FACE + v * UNIT for v in vs]
                return jnp.concatenate([flat[:, c : c + UNIT] for c in cuts], axis=0).astype(BF16)
            left = jnp.dot(units(even), spread_ref[f, :, :half], preferred_element_type=F32)
            right = jnp.dot(units(odd), spread_ref[f, :, half:], preferred_element_type=F32)
            for v in range(NV):
                source, row = (left, v // 2) if v % 2 == 0 else (right, v // 2)
                first = v * VROW // LANES
                for t in range(LEFT_TILES):
                    if first + t >= full.shape[0]:
                        continue
                    value = source[row * slots : (row + 1) * slots, t * LANES : (t + 1) * LANES]
                    at = pl.ds((f + 1) * slots, slots)
                    if v % 2 == 1 and t == 0:
                        full[first + t, at, :] = full[first + t, at, :] + value
                    else:
                        full[first + t, at, :] = value
        n_tiles = full.shape[0]
        for t in range(n_tiles):
            full[t, pl.ds(0, slots), :] = flat[:, DIAG_AT + t * LANES : DIAG_AT + (t + 1) * LANES]

        def emit(slot, carry):
            pieces = [full[t, pl.ds(slot, NFACES + 1, stride=slots), :] for t in range(n_tiles)]
            value = jnp.concatenate(pieces, axis=1).astype(BF16)
            out_ref[slot] = value[:, : out_ref.shape[2]]
            return carry

        lax.fori_loop(0, slots, emit, 0)


def call(kernel, out_shape, scratch, *args, **kwargs):
    return pl.pallas_call(kernel, out_shape=out_shape, scratch_shapes=scratch, **kwargs)(*args)


def shards(diag_jac, xface_jac, side_jac, orient, owner):
    elems = diag_jac.shape[0]
    nf = diag_jac.shape[1]
    length = xface_jac.shape[2]
    pad = round_up(elems, 16)
    grp_size = lax.axis_size("grp")
    slab_size = lax.axis_size("slab")
    owners_n = grp_size // 4
    most = max(2, 3 * elems // (2 * owners_n))
    me = lax.axis_index("grp")
    table = jnp.asarray(face_table())
    right, left = (jnp.asarray(t) for t in diag_tables())

    def by_face(array):
        turned = jnp.transpose(array, (1, 0, 2))
        turned = jnp.pad(turned, ((0, 0), (0, pad - elems), (0, 0)))
        return turned.reshape(-1, length)

    orient_col = jnp.pad(orient, (0, pad - elems))[:, None]
    sds = jax.ShapeDtypeStruct
    plus, sent = call(
        functools.partial(xface_kernel, elems=pad),
        (sds((pad, FACE), BF16), sds((pad, FACE), BF16)),
        [pltpu.VMEM((pad, FACE), F32)],
        by_face(xface_jac), table, jnp.asarray(turn_tables()), orient_col, name="xface",
    )
    minus = lax.ppermute(sent, "slab", [(i, (i + 1) % slab_size) for i in range(slab_size)])
    side = call(
        functools.partial(face_kernel, rows=4 * pad),
        sds((4 * pad, FACE), BF16),
        [pltpu.VMEM((4 * pad, FACE), F32)],
        by_face(side_jac), table, name="side",
    )
    diag = pl.pallas_call(
        functools.partial(diag_kernel, elems=elems),
        grid=(elems,),
        in_specs=[
            pl.BlockSpec((None, nf, nf), lambda e: (e, 0, 0)),
            pl.BlockSpec(right.shape, lambda e: (0, 0)),
            pl.BlockSpec(left.shape, lambda e: (0, 0)),
        ],
        out_specs=pl.BlockSpec((pad, NCOARSE * NCOARSE), lambda e: (0, 0)),
        out_shape=sds((pad, NCOARSE * NCOARSE), BF16),
        scratch_shapes=[pltpu.VMEM((elems * NCOARSE, LANES), F32), pltpu.VMEM((pad, NCOARSE * NCOARSE), F32)],
        name="diag",
    )(diag_jac, right, left)

    earlier = jnp.arange(elems)[None, :] < jnp.arange(elems)[:, None]
    same = owner[:, None] == owner[None, :]
    rank = jnp.sum((same & earlier).astype(jnp.int32), axis=1)
    dest = (owner - me) % owners_n * most + rank
    dest = jnp.pad(dest, (0, pad - elems), constant_values=-1)
    placer = (jnp.arange(owners_n * most, dtype=jnp.int32)[:, None] == dest[None, :]).astype(BF16)
    slot_shape = (owners_n, most, ROW_TILES, LANES)
    packed = call(
        functools.partial(pack_kernel, elems=pad),
        sds(slot_shape, BF16),
        [pltpu.VMEM((pad, ROW_TILES * LANES), F32), pltpu.VMEM((owners_n * most * ROW_TILES, LANES), F32)],
        minus, plus, side, diag, placer, name="pack",
    )
    groups = grp_size // owners_n
    chunks = [packed[0:1]]
    for j in range(1, owners_n):
        pairs = [(a * owners_n + o, a * owners_n + (o + j) % owners_n) for a in range(groups) for o in range(owners_n)]
        chunks.append(lax.ppermute(packed[j : j + 1], "grp", pairs))
    column = jnp.concatenate(chunks, axis=0)
    sources = [column]
    for a in range(1, groups):
        sources.append(lax.ppermute(column, "grp", [(a * owners_n + o, o) for o in range(owners_n)]))

    slots = grp_size * most
    n_tiles = round_up(NCOARSE * NCOARSE, LANES) // LANES
    n_in = len(sources)
    return call(
        functools.partial(unpack_kernel, owners_n=owners_n, most=most),
        sds((slots, NFACES + 1, NCOARSE * NCOARSE), BF16),
        [
            pltpu.VMEM((slots * ROW_TILES, LANES), F32),
            pltpu.VMEM((slots, ROW_TILES * LANES), F32),
            pltpu.VMEM((n_tiles, (NFACES + 1) * slots, LANES), F32),
        ],
        me.astype(jnp.int32)[None], *sources, jnp.asarray(spread_tables()),
        in_specs=[pl.BlockSpec(memory_space=pltpu.SMEM)] + [pl.BlockSpec(memory_space=pltpu.VMEM)] * (n_in + 1),
        name="unpack",
    )


def solution(mesh):
    in_specs = (
        P(("slab", "grp"), None, None),
        P(("slab", "grp"), None, None),
        P(("slab", "grp"), None, None),
        P(("slab", "grp")),
        P(("slab", "grp")),
    )
    out_specs = P(("slab", "grp"), None, None)
    return jax.shard_map(shards, mesh=mesh, in_specs=in_specs, out_specs=out_specs, check_vma=False)
```

```python
import functools

import jax
import jax.numpy as jnp
import numpy as np
from jax import lax
from jax.experimental import pallas as pl
from jax.experimental.pallas import tpu as pltpu
from jax.sharding import PartitionSpec as P


NV = 5
PF = 4
PM = 2
PC = 1
LANES = 128
F32 = jnp.float32
BF16 = jnp.bfloat16


def gll_points(degree):
    if degree == 1:
        return np.array([-1.0, 1.0])
    if degree == 2:
        return np.array([-1.0, 0.0, 1.0])
    inner_pt = np.sqrt(3.0 / 7.0)
    return np.array([-1.0, -inner_pt, 0.0, inner_pt, 1.0])


def lagrange(source_deg, target_deg):
    source = gll_points(source_deg)
    target = gll_points(target_deg)
    result = np.ones((target_deg + 1, source_deg + 1))
    for j in range(source_deg + 1):
        for m in range(source_deg + 1):
            if m != j:
                result[:, j] = result[:, j] * (target - source[m]) / (source[j] - source[m])
    return result


def round_up(value, step):
    return -(-value // step) * step


def split(table):
    leading = table.astype(np.float32).astype(BF16)
    remainder = (table - leading.astype(np.float64)).astype(np.float32).astype(BF16)
    return leading, remainder


LINE = lagrange(PM, PF) @ lagrange(PC, PM)
SIDE = PC + 1
NCOARSE = NV * SIDE**3
PLANE = SIDE**2
UNIT = PLANE * NV * PLANE
FACE = NV * UNIT
VROW = SIDE**3 * NCOARSE
NFACES = 6
DIAG_AT = round_up(NFACES * FACE, LANES)
ROW_TILES = round_up(DIAG_AT + NCOARSE * NCOARSE, LANES) // LANES
LEFT_TILES = round_up(VROW, LANES) // LANES


def face_table():
    face = np.kron(LINE, LINE)
    table = np.kron(face, np.kron(np.eye(NV), face))
    leading, remainder = split(table)
    out = np.zeros((table.shape[0], 2 * LANES), BF16)
    out[:, :UNIT] = leading
    out[:, LANES : LANES + UNIT] = remainder
    return out


def diag_tables():
    table = np.kron(np.eye(NV), np.kron(np.kron(LINE, LINE), LINE))
    leading, remainder = split(table)
    right = np.zeros((table.shape[0], LANES), BF16)
    right[:, :NCOARSE] = leading
    right[:, LANES // 2 : LANES // 2 + NCOARSE] = remainder
    left = np.concatenate([leading.T, remainder.T], axis=0)
    return right, left


def plane_turns():
    flat = np.arange(PLANE)
    first, second = flat // SIDE, flat % SIDE
    tables = []
    for _ in range(4):
        tables.append(first * SIDE + second)
        first, second = SIDE - 1 - second, first
    return tables


def turn_tables():
    out = np.zeros((2, UNIT, 4 * LANES), BF16)
    for o, table in enumerate(plane_turns()):
        for c in range(PLANE):
            for w in range(NV):
                for d in range(PLANE):
                    new = (c * NV + w) * PLANE + d
                    out[0, (c * NV + w) * PLANE + table[d], o * LANES + new] = 1
                    out[1, (table[c] * NV + w) * PLANE + d, o * LANES + new] = 1
    return out


def spread_tables():
    half = VROW % LANES
    out = np.zeros((NFACES, UNIT, 2 * LEFT_TILES * LANES), BF16)

    def full(plane, axis, level):
        pair = [plane // SIDE, plane % SIDE]
        pair.insert(axis, level)
        return (pair[0] * SIDE + pair[1]) * SIDE + pair[2]

    for face in range(NFACES):
        axis, high = face // 2, face % 2
        for c in range(PLANE):
            for w in range(NV):
                for d in range(PLANE):
                    row = full(c, axis, high)
                    col = w * SIDE**3 + full(d, axis, 1 - high)
                    unit = (c * NV + w) * PLANE + d
                    out[face, unit, row * NCOARSE + col] = 1
                    out[face, unit, LEFT_TILES * LANES + half + row * NCOARSE + col] = 1
    return out


def face_kernel(x_ref, table_ref, out_ref, scratch, *, rows):
    width = table_ref.shape[0]
    parts = [x_ref[:, v * width : (v + 1) * width] for v in range(NV)]
    y = jnp.dot(jnp.concatenate(parts, axis=0), table_ref[...], preferred_element_type=F32)
    y = y[:, :LANES] + y[:, LANES:]
    for v in range(NV):
        scratch[:, v * UNIT : (v + 1) * UNIT] = y[v * rows : (v + 1) * rows, :UNIT]
    out_ref[...] = scratch[...].astype(BF16)


def xface_kernel(x_ref, table_ref, turn_ref, orient_ref, plus_ref, sent_ref, scratch, *, elems):
    width = table_ref.shape[0]
    rows = 2 * elems
    parts = [x_ref[:, v * width : (v + 1) * width] for v in range(NV)]
    y = jnp.dot(jnp.concatenate(parts, axis=0), table_ref[...], preferred_element_type=F32)
    y = (y[:, :LANES] + y[:, LANES:])[:, :UNIT].astype(BF16)
    for which, out_ref in enumerate((plus_ref, sent_ref)):
        start = which * elems
        mine = jnp.concatenate([y[v * rows + start : v * rows + start + elems] for v in range(NV)], axis=0)
        turned = jnp.dot(mine, turn_ref[which], preferred_element_type=F32)
        for v in range(NV):
            piece = turned[v * elems : (v + 1) * elems]
            total = jnp.zeros((elems, LANES), F32)
            for o in range(4):
                total = jnp.where(orient_ref[...] == o, piece[:, o * LANES : (o + 1) * LANES], total)
            scratch[:, v * UNIT : (v + 1) * UNIT] = total[:, :UNIT]
        out_ref[...] = scratch[...].astype(BF16)


def coarse_block(block, right, left):
    half = LANES // 2
    y = jnp.dot(block, right, preferred_element_type=F32)
    z = y + pltpu.roll(y, half, 1)
    lane = lax.broadcasted_iota(jnp.int32, z.shape, 1)
    high = z.astype(BF16).astype(F32)
    parts = jnp.where(lane < half, z, z - high).astype(BF16)
    g = jnp.dot(left, parts, preferred_element_type=F32)
    return g[:NCOARSE] + g[NCOARSE:] + pltpu.roll(g[:NCOARSE], half, 1)


def diag_kernel(
    block_ref, right_ref, left_ref, minus_ref, plus_ref, side_ref, placer_ref,
    keep_ref, send_ref, coarse, rows, packed_scr, *, elems, pad,
):
    step = pl.program_id(0)
    many = block_ref.shape[0]
    for i in range(many):
        g = coarse_block(block_ref[i], right_ref[...], left_ref[...])
        coarse[pl.ds((step * many + i) * NCOARSE, NCOARSE), :] = g

    @pl.when(step == 0)
    def _():
        rows[...] = jnp.zeros_like(rows)
        rows[:, :FACE] = minus_ref[...].astype(F32)
        rows[:, FACE : 2 * FACE] = plus_ref[...].astype(F32)
        for f in range(NFACES - 2):
            start = (2 + f) * FACE
            rows[:, start : start + FACE] = side_ref[f * pad : (f + 1) * pad].astype(F32)

    @pl.when(step == pl.num_programs(0) - 1)
    def _():
        for c in range(NCOARSE):
            piece = coarse[pl.ds(c, elems, stride=NCOARSE), :]
            start = DIAG_AT + c * NCOARSE
            rows[:elems, start : start + NCOARSE] = piece[:, :NCOARSE]
        slots = placer_ref.shape[0]
        packed = jnp.dot(placer_ref[...], rows[...].astype(BF16), preferred_element_type=F32)
        for j in range(ROW_TILES):
            packed_scr[pl.ds(j, slots, stride=ROW_TILES), :] = packed[:, j * LANES : (j + 1) * LANES]
        kept = keep_ref.shape[1] * ROW_TILES
        keep_ref[...] = packed_scr[:kept].astype(BF16).reshape(keep_ref.shape)
        send_ref[...] = packed_scr[kept:].astype(BF16).reshape(send_ref.shape)


def unpack_kernel(where_ref, *refs, owners_n, most):
    spread_ref, out_ref, tiles, flat = refs[-4:]
    kept = refs[: (len(refs) - 4) // 2]
    others = refs[(len(refs) - 4) // 2 : -4]
    slots = out_ref.shape[1]
    me = where_ref[0]

    @pl.when(me >= owners_n)
    def _():
        out_ref[...] = jnp.zeros_like(out_ref)

    @pl.when(me < owners_n)
    def _():
        step = most * ROW_TILES
        for a in range(len(kept)):
            for j in range(owners_n):
                chunk = kept[a][0] if j == 0 else others[a][j - 1]
                source = a * owners_n + lax.rem(me - j + owners_n, owners_n)
                tiles[pl.ds(source * step, step), :] = chunk.astype(F32).reshape(step, LANES)
        for j in range(ROW_TILES):
            flat[:, j * LANES : (j + 1) * LANES] = tiles[pl.ds(j, slots, stride=ROW_TILES), :]
        width = NCOARSE * NCOARSE
        out_ref[0] = flat[:, DIAG_AT : DIAG_AT + width].astype(BF16)
        half = LEFT_TILES * LANES
        for f in range(NFACES):
            sums = {}
            for parity in range(2):
                vs = list(range(parity, NV, 2))
                cuts = [f * FACE + v * UNIT for v in vs]
                units = jnp.concatenate([flat[:, c : c + UNIT] for c in cuts], axis=0).astype(BF16)
                table = spread_ref[f, :, parity * half : (parity + 1) * half]
                spread = jnp.dot(units, table, preferred_element_type=F32)
                for row, v in enumerate(vs):
                    for t in range(LEFT_TILES):
                        tile = v * VROW // LANES + t
                        if tile * LANES >= width:
                            continue
                        value = spread[row * slots : (row + 1) * slots, t * LANES : (t + 1) * LANES]
                        sums[tile] = sums[tile] + value if tile in sums else value
            for tile, value in sums.items():
                cut = min(LANES, width - tile * LANES)
                out_ref[f + 1, :, tile * LANES : tile * LANES + cut] = value[:, :cut].astype(BF16)


def call(kernel, out_shape, scratch, *args, **kwargs):
    return pl.pallas_call(kernel, out_shape=out_shape, scratch_shapes=scratch, **kwargs)(*args)


def shards(diag_jac, xface_jac, side_jac, orient, owner):
    elems = diag_jac.shape[0]
    nf = diag_jac.shape[1]
    length = xface_jac.shape[2]
    pad = round_up(elems, 16)
    grp_size = lax.axis_size("grp")
    slab_size = lax.axis_size("slab")
    owners_n = grp_size // 4
    most = max(2, 3 * elems // (2 * owners_n))
    me = lax.axis_index("grp")
    table = jnp.asarray(face_table())
    right, left = (jnp.asarray(t) for t in diag_tables())

    def by_face(array):
        turned = jnp.transpose(array, (1, 0, 2))
        turned = jnp.pad(turned, ((0, 0), (0, pad - elems), (0, 0)))
        return turned.reshape(-1, length)

    orient_col = jnp.pad(orient, (0, pad - elems))[:, None]
    sds = jax.ShapeDtypeStruct
    plus, sent = call(
        functools.partial(xface_kernel, elems=pad),
        (sds((pad, FACE), BF16), sds((pad, FACE), BF16)),
        [pltpu.VMEM((pad, FACE), F32)],
        by_face(xface_jac), table, jnp.asarray(turn_tables()), orient_col, name="xface",
    )
    minus = lax.ppermute(sent, "slab", [(i, (i + 1) % slab_size) for i in range(slab_size)])
    side = call(
        functools.partial(face_kernel, rows=4 * pad),
        sds((4 * pad, FACE), BF16),
        [pltpu.VMEM((4 * pad, FACE), F32)],
        by_face(side_jac), table, name="side",
    )
    earlier = jnp.arange(elems)[None, :] < jnp.arange(elems)[:, None]
    same = owner[:, None] == owner[None, :]
    rank = jnp.sum((same & earlier).astype(jnp.int32), axis=1)
    dest = (owner - me) % owners_n * most + rank
    dest = jnp.pad(dest, (0, pad - elems), constant_values=-1)
    placer = (jnp.arange(owners_n * most, dtype=jnp.int32)[:, None] == dest[None, :]).astype(BF16)

    many = max(n for n in range(1, 4) if elems % n == 0)
    small = [right, left, minus, plus, side, placer]
    chunk = (most, ROW_TILES, LANES)
    keep, send = pl.pallas_call(
        functools.partial(diag_kernel, elems=elems, pad=pad),
        grid=(elems // many,),
        in_specs=[pl.BlockSpec((many, nf, nf), lambda e: (e, 0, 0))]
        + [pl.BlockSpec(array.shape, lambda e: (0, 0)) for array in small],
        out_specs=[
            pl.BlockSpec((1,) + chunk, lambda e: (0, 0, 0, 0)),
            pl.BlockSpec((owners_n - 1,) + chunk, lambda e: (0, 0, 0, 0)),
        ],
        out_shape=[sds((1,) + chunk, BF16), sds((owners_n - 1,) + chunk, BF16)],
        scratch_shapes=[
            pltpu.VMEM((elems * NCOARSE, LANES), F32),
            pltpu.VMEM((pad, ROW_TILES * LANES), F32),
            pltpu.VMEM((owners_n * most * ROW_TILES, LANES), F32),
        ],
        name="diag",
    )(diag_jac, *small)

    groups = grp_size // owners_n
    arrived = []
    for j in range(1, owners_n):
        pairs = [(a * owners_n + o, a * owners_n + (o + j) % owners_n) for a in range(groups) for o in range(owners_n)]
        arrived.append(lax.ppermute(send[j - 1 : j], "grp", pairs))
    arrived = jnp.concatenate(arrived, axis=0) if len(arrived) > 1 else arrived[0]

    def to_owners(array):
        return [array] + [
            lax.ppermute(array, "grp", [(a * owners_n + o, o) for o in range(owners_n)]) for a in range(1, groups)
        ]

    kept = to_owners(keep)
    others = to_owners(arrived)
    sources = kept + others

    slots = grp_size * most
    rows = call(
        functools.partial(unpack_kernel, owners_n=owners_n, most=most),
        sds((NFACES + 1, slots, NCOARSE * NCOARSE), BF16),
        [pltpu.VMEM((slots * ROW_TILES, LANES), F32), pltpu.VMEM((slots, ROW_TILES * LANES), F32)],
        me.astype(jnp.int32)[None], *sources, jnp.asarray(spread_tables()),
        in_specs=[pl.BlockSpec(memory_space=pltpu.SMEM)] + [pl.BlockSpec(memory_space=pltpu.VMEM)] * (len(sources) + 1),
        name="unpack",
    )
    return jnp.transpose(rows, (1, 0, 2))


def solution(mesh):
    in_specs = (
        P(("slab", "grp"), None, None),
        P(("slab", "grp"), None, None),
        P(("slab", "grp"), None, None),
        P(("slab", "grp")),
        P(("slab", "grp")),
    )
    out_specs = P(("slab", "grp"), None, None)
    return jax.shard_map(shards, mesh=mesh, in_specs=in_specs, out_specs=out_specs, check_vma=False)
```

```python
import functools

import jax
import jax.numpy as jnp
import numpy as np
from jax import lax
from jax.experimental import pallas as pl
from jax.experimental.pallas import tpu as pltpu
from jax.sharding import PartitionSpec as P


NV = 5
PF = 4
PM = 2
PC = 1
LANES = 128
F32 = jnp.float32
BF16 = jnp.bfloat16
VMEM = pl.BlockSpec(memory_space=pltpu.VMEM)
SMALL = pl.BlockSpec(memory_space=pltpu.SMEM)


def gll_points(degree):
    if degree == 1:
        return np.array([-1.0, 1.0])
    if degree == 2:
        return np.array([-1.0, 0.0, 1.0])
    inner_pt = np.sqrt(3.0 / 7.0)
    return np.array([-1.0, -inner_pt, 0.0, inner_pt, 1.0])


def lagrange(source_deg, target_deg):
    source = gll_points(source_deg)
    target = gll_points(target_deg)
    result = np.ones((target_deg + 1, source_deg + 1))
    for j in range(source_deg + 1):
        for m in range(source_deg + 1):
            if m != j:
                result[:, j] = result[:, j] * (target - source[m]) / (source[j] - source[m])
    return result


def round_up(value, step):
    return -(-value // step) * step


def split(table):
    leading = table.astype(np.float32).astype(BF16)
    remainder = (table - leading.astype(np.float64)).astype(np.float32).astype(BF16)
    return leading, remainder


LINE = lagrange(PM, PF) @ lagrange(PC, PM)
SIDE = PC + 1
NCOARSE = NV * SIDE**3
PLANE = SIDE**2
UNIT = PLANE * NV * PLANE
FACE = NV * UNIT
VROW = SIDE**3 * NCOARSE
NFACES = 6
DIAG_AT = round_up(NFACES * FACE, LANES)
ROW_TILES = round_up(DIAG_AT + NCOARSE * NCOARSE, LANES) // LANES
LEFT_TILES = round_up(VROW, LANES) // LANES


def face_table():
    face = np.kron(LINE, LINE)
    table = np.kron(face, np.kron(np.eye(NV), face))
    leading, remainder = split(table)
    out = np.zeros((table.shape[0], 2 * LANES), BF16)
    out[:, :UNIT] = leading
    out[:, LANES : LANES + UNIT] = remainder
    return out


def diag_tables():
    table = np.kron(np.eye(NV), np.kron(np.kron(LINE, LINE), LINE))
    leading, remainder = split(table)
    right = np.zeros((table.shape[0], LANES), BF16)
    right[:, :NCOARSE] = leading
    right[:, LANES // 2 : LANES // 2 + NCOARSE] = remainder
    left = np.concatenate([leading.T, remainder.T], axis=0)
    return right, left


def plane_turns():
    flat = np.arange(PLANE)
    first, second = flat // SIDE, flat % SIDE
    tables = []
    for _ in range(4):
        tables.append(first * SIDE + second)
        first, second = SIDE - 1 - second, first
    return tables


def turn_tables():
    out = np.zeros((2, UNIT, 4 * LANES), BF16)
    for o, table in enumerate(plane_turns()):
        for c in range(PLANE):
            for w in range(NV):
                for d in range(PLANE):
                    new = (c * NV + w) * PLANE + d
                    out[0, (c * NV + w) * PLANE + table[d], o * LANES + new] = 1
                    out[1, (table[c] * NV + w) * PLANE + d, o * LANES + new] = 1
    return out


def spread_tables():
    half = VROW % LANES
    out = np.zeros((NFACES, UNIT, 2 * LEFT_TILES * LANES), BF16)

    def full(plane, axis, level):
        pair = [plane // SIDE, plane % SIDE]
        pair.insert(axis, level)
        return (pair[0] * SIDE + pair[1]) * SIDE + pair[2]

    for face in range(NFACES):
        axis, high = face // 2, face % 2
        for c in range(PLANE):
            for w in range(NV):
                for d in range(PLANE):
                    row = full(c, axis, high)
                    col = w * SIDE**3 + full(d, axis, 1 - high)
                    unit = (c * NV + w) * PLANE + d
                    out[face, unit, row * NCOARSE + col] = 1
                    out[face, unit, LEFT_TILES * LANES + half + row * NCOARSE + col] = 1
    return out


def face_kernel(x_ref, table_ref, out_ref, scratch, *, rows):
    width = table_ref.shape[0]
    parts = [x_ref[:, v * width : (v + 1) * width] for v in range(NV)]
    y = jnp.dot(jnp.concatenate(parts, axis=0), table_ref[...], preferred_element_type=F32)
    y = y[:, :LANES] + y[:, LANES:]
    for v in range(NV):
        scratch[:, v * UNIT : (v + 1) * UNIT] = y[v * rows : (v + 1) * rows, :UNIT]
    out_ref[...] = scratch[...].astype(BF16)


def as_column(row, count):
    shape = (count, row.shape[1])
    diagonal = lax.broadcasted_iota(jnp.int32, shape, 0) == lax.broadcasted_iota(jnp.int32, shape, 1)
    return jnp.sum(jnp.where(diagonal, row, 0), axis=1, keepdims=True)


def placement(owner, me, owners_n, most):
    elems = owner.shape[1]
    shape = (elems, elems)
    earlier = lax.broadcasted_iota(jnp.int32, shape, 0) < lax.broadcasted_iota(jnp.int32, shape, 1)
    same = as_column(owner, elems) == owner
    rank = jnp.sum(jnp.where(same & earlier, 1, 0), axis=0, keepdims=True)
    dest = lax.rem(owner - lax.rem(me, owners_n) + owners_n, owners_n) * most + rank
    slot = lax.broadcasted_iota(jnp.int32, (owners_n * most, elems), 0)
    return jnp.where(slot == dest, 1.0, 0.0).astype(BF16)


def xface_kernel(x_ref, table_ref, turn_ref, orient_ref, plus_ref, sent_ref, scratch, *, elems):
    width = table_ref.shape[0]
    rows = 2 * elems
    parts = [x_ref[:, v * width : (v + 1) * width] for v in range(NV)]
    y = jnp.dot(jnp.concatenate(parts, axis=0), table_ref[...], preferred_element_type=F32)
    y = (y[:, :LANES] + y[:, LANES:])[:, :UNIT].astype(BF16)
    orient = as_column(orient_ref[...], elems)
    for which, out_ref in enumerate((plus_ref, sent_ref)):
        start = which * elems
        mine = jnp.concatenate([y[v * rows + start : v * rows + start + elems] for v in range(NV)], axis=0)
        turned = jnp.dot(mine, turn_ref[which], preferred_element_type=F32)
        for v in range(NV):
            piece = turned[v * elems : (v + 1) * elems]
            total = jnp.zeros((elems, LANES), F32)
            for o in range(4):
                total = jnp.where(orient == o, piece[:, o * LANES : (o + 1) * LANES], total)
            scratch[:, v * UNIT : (v + 1) * UNIT] = total[:, :UNIT]
        out_ref[...] = scratch[...].astype(BF16)


def coarse_block(block, right, left):
    half = LANES // 2
    y = jnp.dot(block, right, preferred_element_type=F32)
    z = y + pltpu.roll(y, half, 1)
    lane = lax.broadcasted_iota(jnp.int32, z.shape, 1)
    high = z.astype(BF16).astype(F32)
    parts = jnp.where(lane < half, z, z - high).astype(BF16)
    g = jnp.dot(left, parts, preferred_element_type=F32)
    return g[:NCOARSE] + g[NCOARSE:] + pltpu.roll(g[:NCOARSE], half, 1)


def diag_kernel(
    block_ref, where_ref, right_ref, left_ref, minus_ref, plus_ref, side_ref, owner_ref,
    keep_ref, send_ref, coarse, rows, packed_scr, *, elems, pad, owners_n,
):
    step = pl.program_id(0)
    many = block_ref.shape[0]
    for i in range(many):
        g = coarse_block(block_ref[i], right_ref[...], left_ref[...])
        coarse[pl.ds((step * many + i) * NCOARSE, NCOARSE), :] = g

    @pl.when(step == 0)
    def _():
        rows[...] = jnp.zeros_like(rows)
        rows[:, :FACE] = minus_ref[...].astype(F32)
        rows[:, FACE : 2 * FACE] = plus_ref[...].astype(F32)
        for f in range(NFACES - 2):
            start = (2 + f) * FACE
            rows[:, start : start + FACE] = side_ref[f * pad : (f + 1) * pad].astype(F32)

    @pl.when(step == pl.num_programs(0) - 1)
    def _():
        for c in range(NCOARSE):
            piece = coarse[pl.ds(c, elems, stride=NCOARSE), :]
            start = DIAG_AT + c * NCOARSE
            rows[:elems, start : start + NCOARSE] = piece[:, :NCOARSE]
        most = keep_ref.shape[1]
        slots = owners_n * most
        placer = placement(owner_ref[...], where_ref[0], owners_n, most)
        packed = jnp.dot(placer, rows[:elems].astype(BF16), preferred_element_type=F32)
        for j in range(ROW_TILES):
            packed_scr[pl.ds(j, slots, stride=ROW_TILES), :] = packed[:, j * LANES : (j + 1) * LANES]
        kept = most * ROW_TILES
        keep_ref[...] = packed_scr[:kept].astype(BF16).reshape(keep_ref.shape)
        send_ref[...] = packed_scr[kept:].astype(BF16).reshape(send_ref.shape)


def unpack_kernel(where_ref, *refs, owners_n, most):
    spread_ref, out_ref, tiles, flat = refs[-4:]
    kept = refs[: (len(refs) - 4) // 2]
    others = refs[(len(refs) - 4) // 2 : -4]
    slots = out_ref.shape[1]
    me = where_ref[0]

    @pl.when(me >= owners_n)
    def _():
        out_ref[...] = jnp.zeros_like(out_ref)

    width = NCOARSE * NCOARSE
    half = LEFT_TILES * LANES
    block = pl.program_id(0)

    @pl.when((me < owners_n) & (block == 0))
    def _():
        step = most * ROW_TILES
        for a in range(len(kept)):
            for j in range(owners_n):
                chunk = kept[a][0] if j == 0 else others[a][j - 1]
                source = a * owners_n + lax.rem(me - j + owners_n, owners_n)
                tiles[pl.ds(source * step, step), :] = chunk.astype(F32).reshape(step, LANES)
        for j in range(ROW_TILES):
            flat[:, j * LANES : (j + 1) * LANES] = tiles[pl.ds(j, slots, stride=ROW_TILES), :]
        out_ref[0] = flat[:, DIAG_AT : DIAG_AT + width].astype(BF16)

    def spread_face(f):
        sums = {}
        for parity in range(2):
            vs = list(range(parity, NV, 2))
            cuts = [f * FACE + v * UNIT for v in vs]
            units = jnp.concatenate([flat[:, c : c + UNIT] for c in cuts], axis=0).astype(BF16)
            table = spread_ref[f, :, parity * half : (parity + 1) * half]
            spread = jnp.dot(units, table, preferred_element_type=F32)
            for row, v in enumerate(vs):
                for t in range(LEFT_TILES):
                    tile = v * VROW // LANES + t
                    if tile * LANES >= width:
                        continue
                    value = spread[row * slots : (row + 1) * slots, t * LANES : (t + 1) * LANES]
                    sums[tile] = sums[tile] + value if tile in sums else value
        for tile, value in sums.items():
            cut = min(LANES, width - tile * LANES)
            out_ref[0, :, tile * LANES : tile * LANES + cut] = value[:, :cut].astype(BF16)

    for f in range(NFACES):
        pl.when((me < owners_n) & (block == f + 1))(functools.partial(spread_face, f))


def call(kernel, out_shape, scratch, *args, **kwargs):
    return pl.pallas_call(kernel, out_shape=out_shape, scratch_shapes=scratch, **kwargs)(*args)


def shards(diag_jac, xface_jac, side_jac, orient, owner):
    elems = diag_jac.shape[0]
    nf = diag_jac.shape[1]
    length = xface_jac.shape[2]
    pad = round_up(elems, 16)
    grp_size = lax.axis_size("grp")
    slab_size = lax.axis_size("slab")
    owners_n = grp_size // 4
    most = max(2, 3 * elems // (2 * owners_n))
    where = lax.axis_index("grp").astype(jnp.int32)[None]
    table = jnp.asarray(face_table())
    right, left = (jnp.asarray(t) for t in diag_tables())

    def by_face(array):
        turned = jnp.transpose(array, (1, 0, 2))
        turned = jnp.pad(turned, ((0, 0), (0, pad - elems), (0, 0)))
        return turned.reshape(-1, length)

    sds = jax.ShapeDtypeStruct
    plus, sent = call(
        functools.partial(xface_kernel, elems=pad),
        (sds((pad, FACE), BF16), sds((pad, FACE), BF16)),
        [pltpu.VMEM((pad, FACE), F32)],
        by_face(xface_jac), table, jnp.asarray(turn_tables()), orient[None, :],
        in_specs=[VMEM] * 4, out_specs=(VMEM, VMEM), name="xface",
    )
    minus = lax.ppermute(sent, "slab", [(i, (i + 1) % slab_size) for i in range(slab_size)])
    side = call(
        functools.partial(face_kernel, rows=4 * pad),
        sds((4 * pad, FACE), BF16),
        [pltpu.VMEM((4 * pad, FACE), F32)],
        by_face(side_jac), table,
        in_specs=[VMEM] * 2, out_specs=VMEM, name="side",
    )
    many = max(n for n in range(1, 4) if elems % n == 0)
    small = [right, left, minus, plus, side, owner[None, :]]
    chunk = (most, ROW_TILES, LANES)
    keep, send = pl.pallas_call(
        functools.partial(diag_kernel, elems=elems, pad=pad, owners_n=owners_n),
        grid=(elems // many,),
        in_specs=[pl.BlockSpec((many, nf, nf), lambda e: (e, 0, 0)), SMALL] + [VMEM] * len(small),
        out_specs=[
            pl.BlockSpec((1,) + chunk, lambda e: (0, 0, 0, 0)),
            pl.BlockSpec((owners_n - 1,) + chunk, lambda e: (0, 0, 0, 0)),
        ],
        out_shape=[sds((1,) + chunk, BF16), sds((owners_n - 1,) + chunk, BF16)],
        scratch_shapes=[
            pltpu.VMEM((elems * NCOARSE, LANES), F32),
            pltpu.VMEM((pad, ROW_TILES * LANES), F32),
            pltpu.VMEM((owners_n * most * ROW_TILES, LANES), F32),
        ],
        name="diag",
    )(diag_jac, where, *small)

    groups = grp_size // owners_n
    arrived = []
    for j in range(1, owners_n):
        pairs = [(a * owners_n + o, a * owners_n + (o + j) % owners_n) for a in range(groups) for o in range(owners_n)]
        arrived.append(lax.ppermute(send[j - 1 : j], "grp", pairs))
    arrived = jnp.concatenate(arrived, axis=0) if len(arrived) > 1 else arrived[0]

    def exchange(a):
        place = list(range(grp_size))
        for o in range(owners_n):
            place[o], place[a * owners_n + o] = a * owners_n + o, o
        return list(enumerate(place))

    def to_owners(array):
        return [array] + [lax.ppermute(array, "grp", exchange(a)) for a in range(1, groups)]

    kept = to_owners(keep)
    others = to_owners(arrived)
    sources = kept + others

    slots = grp_size * most
    rows = call(
        functools.partial(unpack_kernel, owners_n=owners_n, most=most),
        sds((NFACES + 1, slots, NCOARSE * NCOARSE), BF16),
        [pltpu.VMEM((slots * ROW_TILES, LANES), F32), pltpu.VMEM((slots, ROW_TILES * LANES), F32)],
        where, *sources, jnp.asarray(spread_tables()),
        grid=(NFACES + 1,),
        in_specs=[SMALL] + [VMEM] * (len(sources) + 1),
        out_specs=pl.BlockSpec((1, slots, NCOARSE * NCOARSE), lambda i: (i, 0, 0)),
        name="unpack",
    )
    return jnp.transpose(rows, (1, 0, 2))


def solution(mesh):
    in_specs = (
        P(("slab", "grp"), None, None),
        P(("slab", "grp"), None, None),
        P(("slab", "grp"), None, None),
        P(("slab", "grp")),
        P(("slab", "grp")),
    )
    out_specs = P(("slab", "grp"), None, None)
    return jax.shard_map(shards, mesh=mesh, in_specs=in_specs, out_specs=out_specs, check_vma=False)
```

```python
import functools

import jax
import jax.numpy as jnp
import numpy as np
from jax import lax
from jax.experimental import pallas as pl
from jax.experimental.pallas import tpu as pltpu
from jax.sharding import PartitionSpec as P


NV = 5
PF = 4
PM = 2
PC = 1
LANES = 128
F32 = jnp.float32
BF16 = jnp.bfloat16
VMEM = pl.BlockSpec(memory_space=pltpu.VMEM)
SMALL = pl.BlockSpec(memory_space=pltpu.SMEM)


def gll_points(degree):
    if degree == 1:
        return np.array([-1.0, 1.0])
    if degree == 2:
        return np.array([-1.0, 0.0, 1.0])
    inner_pt = np.sqrt(3.0 / 7.0)
    return np.array([-1.0, -inner_pt, 0.0, inner_pt, 1.0])


def lagrange(source_deg, target_deg):
    source = gll_points(source_deg)
    target = gll_points(target_deg)
    result = np.ones((target_deg + 1, source_deg + 1))
    for j in range(source_deg + 1):
        for m in range(source_deg + 1):
            if m != j:
                result[:, j] = result[:, j] * (target - source[m]) / (source[j] - source[m])
    return result


def round_up(value, step):
    return -(-value // step) * step


def split(table):
    leading = table.astype(np.float32).astype(BF16)
    remainder = (table - leading.astype(np.float64)).astype(np.float32).astype(BF16)
    return leading, remainder


LINE = lagrange(PM, PF) @ lagrange(PC, PM)
SIDE = PC + 1
NCOARSE = NV * SIDE**3
PLANE = SIDE**2
UNIT = PLANE * NV * PLANE
FACE = NV * UNIT
VROW = SIDE**3 * NCOARSE
NFACES = 6
DIAG_AT = round_up(NFACES * FACE, LANES)
ROW_TILES = round_up(DIAG_AT + NCOARSE * NCOARSE, LANES) // LANES
LEFT_TILES = round_up(VROW, LANES) // LANES


def face_table():
    face = np.kron(LINE, LINE)
    table = np.kron(face, np.kron(np.eye(NV), face))
    leading, remainder = split(table)
    out = np.zeros((table.shape[0], 2 * LANES), BF16)
    out[:, :UNIT] = leading
    out[:, LANES : LANES + UNIT] = remainder
    return out


def diag_tables():
    table = np.kron(np.eye(NV), np.kron(np.kron(LINE, LINE), LINE))
    leading, remainder = split(table)
    right = np.zeros((table.shape[0], LANES), BF16)
    right[:, :NCOARSE] = leading
    right[:, LANES // 2 : LANES // 2 + NCOARSE] = remainder
    left = np.concatenate([leading.T, remainder.T], axis=0)
    return right, left


def plane_turns():
    flat = np.arange(PLANE)
    first, second = flat // SIDE, flat % SIDE
    tables = []
    for _ in range(4):
        tables.append(first * SIDE + second)
        first, second = SIDE - 1 - second, first
    return tables


def turn_tables():
    out = np.zeros((2, UNIT, 4 * LANES), BF16)
    for o, table in enumerate(plane_turns()):
        for c in range(PLANE):
            for w in range(NV):
                for d in range(PLANE):
                    new = (c * NV + w) * PLANE + d
                    out[0, (c * NV + w) * PLANE + table[d], o * LANES + new] = 1
                    out[1, (table[c] * NV + w) * PLANE + d, o * LANES + new] = 1
    return out


def spread_tables():
    half = VROW % LANES
    out = np.zeros((NFACES, UNIT, 2 * LEFT_TILES * LANES), BF16)

    def full(plane, axis, level):
        pair = [plane // SIDE, plane % SIDE]
        pair.insert(axis, level)
        return (pair[0] * SIDE + pair[1]) * SIDE + pair[2]

    for face in range(NFACES):
        axis, high = face // 2, face % 2
        for c in range(PLANE):
            for w in range(NV):
                for d in range(PLANE):
                    row = full(c, axis, high)
                    col = w * SIDE**3 + full(d, axis, 1 - high)
                    unit = (c * NV + w) * PLANE + d
                    out[face, unit, row * NCOARSE + col] = 1
                    out[face, unit, LEFT_TILES * LANES + half + row * NCOARSE + col] = 1
    return out


def face_product(x, table, stacked, products):
    width = table.shape[0]
    count = x.shape[0]
    pitch = stacked.shape[0] // NV
    for v in range(NV):
        stacked[v * pitch : v * pitch + count, :] = x[:, v * width : (v + 1) * width]
        if pitch > count:
            stacked[v * pitch + count : (v + 1) * pitch, :] = jnp.zeros((pitch - count, width), BF16)
    y = jnp.dot(stacked[...], table[...], preferred_element_type=F32)
    products[...] = y[:, :LANES] + y[:, LANES:]


def as_column(row, count):
    shape = (count, row.shape[1])
    diagonal = lax.broadcasted_iota(jnp.int32, shape, 0) == lax.broadcasted_iota(jnp.int32, shape, 1)
    return jnp.sum(jnp.where(diagonal, row, 0), axis=1, keepdims=True)


def placement(owner, me, owners_n, most):
    elems = owner.shape[1]
    shape = (elems, elems)
    earlier = lax.broadcasted_iota(jnp.int32, shape, 0) < lax.broadcasted_iota(jnp.int32, shape, 1)
    same = as_column(owner, elems) == owner
    rank = jnp.sum(jnp.where(same & earlier, 1, 0), axis=0, keepdims=True)
    dest = lax.rem(owner - lax.rem(me, owners_n) + owners_n, owners_n) * most + rank
    slot = lax.broadcasted_iota(jnp.int32, (owners_n * most, elems), 0)
    return jnp.where(slot == dest, 1.0, 0.0).astype(BF16)


def xface_kernel(x_ref, table_ref, turn_ref, orient_ref, plus_ref, sent_ref, stacked, products, scratch):
    face_product(x_ref, table_ref, stacked, products)
    pitch = stacked.shape[0] // NV
    elems = pitch // 2
    orient = as_column(orient_ref[...], elems)
    for which, out_ref in enumerate((plus_ref, sent_ref)):
        units = [products[pl.ds(v * pitch + which, elems, stride=2), :] for v in range(NV)]
        mine = jnp.concatenate(units, axis=0)[:, :UNIT].astype(BF16)
        turned = jnp.dot(mine, turn_ref[which], preferred_element_type=F32)
        for v in range(NV):
            piece = turned[v * elems : (v + 1) * elems]
            total = jnp.zeros((elems, LANES), F32)
            for o in range(4):
                total = jnp.where(orient == o, piece[:, o * LANES : (o + 1) * LANES], total)
            scratch[:, v * UNIT : (v + 1) * UNIT] = total[:, :UNIT]
        out_ref[...] = scratch[...].astype(BF16)


def coarse_block(block, right, left):
    half = LANES // 2
    y = jnp.dot(block, right, preferred_element_type=F32)
    z = y + pltpu.roll(y, half, 1)
    lane = lax.broadcasted_iota(jnp.int32, z.shape, 1)
    high = z.astype(BF16).astype(F32)
    parts = jnp.where(lane < half, z, z - high).astype(BF16)
    g = jnp.dot(left, parts, preferred_element_type=F32)
    return g[:NCOARSE] + g[NCOARSE:] + pltpu.roll(g[:NCOARSE], half, 1)


def main_kernel(
    where_ref, diag_hbm, side_hbm, table_hbm, right_ref, left_ref, minus_ref, plus_ref, owner_ref,
    keep_ref, send_ref, blocks, side, table, stacked, products, coarse, rows, packed_scr, sems, *, many, owners_n,
):
    elems = blocks.shape[0]
    n_side = side.shape[0] // elems
    side_copy = pltpu.make_async_copy(side_hbm, side, sems.at[elems])
    table_copy = pltpu.make_async_copy(table_hbm, table, sems.at[elems + 1])

    def block_copy(e):
        return pltpu.make_async_copy(diag_hbm.at[e], blocks.at[e], sems.at[e])

    side_copy.start()
    table_copy.start()
    for e in range(elems):
        block_copy(e).start()
    rows[...] = jnp.zeros_like(rows)
    rows[:, :FACE] = minus_ref[...].astype(F32)
    rows[:, FACE : 2 * FACE] = plus_ref[...].astype(F32)
    side_copy.wait()
    table_copy.wait()
    face_product(side, table, stacked, products)
    pitch = stacked.shape[0] // NV
    for f in range(n_side):
        for v in range(NV):
            start = (2 + f) * FACE + v * UNIT
            unit = products[pl.ds(v * pitch + f, elems, stride=n_side), :]
            rows[:elems, start : start + UNIT] = unit[:, :UNIT]

    def some_blocks(step, carry):
        for i in range(many):
            block_copy(step * many + i).wait()
        for i in range(many):
            e = step * many + i
            g = coarse_block(blocks[e], right_ref[...], left_ref[...])
            coarse[pl.ds(e * NCOARSE, NCOARSE), :] = g
        return carry

    lax.fori_loop(0, elems // many, some_blocks, 0)
    for c in range(NCOARSE):
        piece = coarse[pl.ds(c, elems, stride=NCOARSE), :]
        start = DIAG_AT + c * NCOARSE
        rows[:elems, start : start + NCOARSE] = piece[:, :NCOARSE]
    most = keep_ref.shape[1]
    slots = owners_n * most
    placer = placement(owner_ref[...], where_ref[0], owners_n, most)
    packed = jnp.dot(placer, rows[:elems].astype(BF16), preferred_element_type=F32)
    for j in range(ROW_TILES):
        packed_scr[pl.ds(j, slots, stride=ROW_TILES), :] = packed[:, j * LANES : (j + 1) * LANES]
    kept = most * ROW_TILES
    keep_ref[...] = packed_scr[:kept].astype(BF16).reshape(keep_ref.shape)
    send_ref[...] = packed_scr[kept:].astype(BF16).reshape(send_ref.shape)


def unpack_kernel(where_ref, *refs, owners_n, most):
    spread_ref, out_ref, tiles, flat = refs[-4:]
    kept = refs[: (len(refs) - 4) // 2]
    others = refs[(len(refs) - 4) // 2 : -4]
    slots = out_ref.shape[1]
    me = where_ref[0]

    @pl.when(me >= owners_n)
    def _():
        out_ref[...] = jnp.zeros_like(out_ref)

    @pl.when(me < owners_n)
    def _():
        step = most * ROW_TILES
        for a in range(len(kept)):
            for j in range(owners_n):
                chunk = kept[a][0] if j == 0 else others[a][j - 1]
                source = a * owners_n + lax.rem(me - j + owners_n, owners_n)
                tiles[pl.ds(source * step, step), :] = chunk.astype(F32).reshape(step, LANES)
        for j in range(ROW_TILES):
            flat[:, j * LANES : (j + 1) * LANES] = tiles[pl.ds(j, slots, stride=ROW_TILES), :]
        width = NCOARSE * NCOARSE
        out_ref[0] = flat[:, DIAG_AT : DIAG_AT + width].astype(BF16)
        half = LEFT_TILES * LANES
        for f in range(NFACES):
            sums = {}
            for parity in range(2):
                vs = list(range(parity, NV, 2))
                cuts = [f * FACE + v * UNIT for v in vs]
                units = jnp.concatenate([flat[:, c : c + UNIT] for c in cuts], axis=0).astype(BF16)
                table = spread_ref[f, :, parity * half : (parity + 1) * half]
                spread = jnp.dot(units, table, preferred_element_type=F32)
                for row, v in enumerate(vs):
                    for t in range(LEFT_TILES):
                        tile = v * VROW // LANES + t
                        if tile * LANES >= width:
                            continue
                        value = spread[row * slots : (row + 1) * slots, t * LANES : (t + 1) * LANES]
                        sums[tile] = sums[tile] + value if tile in sums else value
            for tile, value in sums.items():
                cut = min(LANES, width - tile * LANES)
                out_ref[f + 1, :, tile * LANES : tile * LANES + cut] = value[:, :cut].astype(BF16)


def call(kernel, out_shape, scratch, *args, **kwargs):
    return pl.pallas_call(kernel, out_shape=out_shape, scratch_shapes=scratch, **kwargs)(*args)


def shards(diag_jac, xface_jac, side_jac, orient, owner):
    elems = diag_jac.shape[0]
    nf = diag_jac.shape[1]
    length = xface_jac.shape[2]
    pad = round_up(elems, 16)
    grp_size = lax.axis_size("grp")
    slab_size = lax.axis_size("slab")
    owners_n = grp_size // 4
    most = max(2, 3 * elems // (2 * owners_n))
    where = lax.axis_index("grp").astype(jnp.int32)[None]
    table = jnp.asarray(face_table())
    right, left = (jnp.asarray(t) for t in diag_tables())

    sds = jax.ShapeDtypeStruct
    width = table.shape[0]
    plus, sent = call(
        xface_kernel,
        (sds((pad, FACE), BF16), sds((pad, FACE), BF16)),
        [
            pltpu.VMEM((NV * 2 * pad, width), BF16),
            pltpu.VMEM((NV * 2 * pad, LANES), F32),
            pltpu.VMEM((pad, FACE), F32),
        ],
        xface_jac.reshape(2 * elems, length), table, jnp.asarray(turn_tables()), orient[None, :], name="xface",
    )
    minus = lax.ppermute(sent, "slab", [(i, (i + 1) % slab_size) for i in range(slab_size)])

    many = max(n for n in range(1, 4) if elems % n == 0)
    n_side = side_jac.shape[1]
    pitch = round_up(n_side * elems, 16)
    chunk = (most, ROW_TILES, LANES)
    keep, send = call(
        functools.partial(main_kernel, many=many, owners_n=owners_n),
        (sds((1,) + chunk, BF16), sds((owners_n - 1,) + chunk, BF16)),
        [
            pltpu.VMEM((elems, nf, nf), BF16),
            pltpu.VMEM((n_side * elems, length), BF16),
            pltpu.VMEM(table.shape, BF16),
            pltpu.VMEM((NV * pitch, width), BF16),
            pltpu.VMEM((NV * pitch, LANES), F32),
            pltpu.VMEM((elems * NCOARSE, LANES), F32),
            pltpu.VMEM((pad, ROW_TILES * LANES), F32),
            pltpu.VMEM((owners_n * most * ROW_TILES, LANES), F32),
            pltpu.SemaphoreType.DMA((elems + 2,)),
        ],
        where, diag_jac, side_jac.reshape(n_side * elems, length), table, right, left, minus, plus, owner[None, :],
        in_specs=[SMALL] + [pl.BlockSpec(memory_space=pl.ANY)] * 3 + [VMEM] * 5,
        name="main",
    )

    groups = grp_size // owners_n
    arrived = []
    for j in range(1, owners_n):
        pairs = [(a * owners_n + o, a * owners_n + (o + j) % owners_n) for a in range(groups) for o in range(owners_n)]
        arrived.append(lax.ppermute(send[j - 1 : j], "grp", pairs))
    arrived = jnp.concatenate(arrived, axis=0) if len(arrived) > 1 else arrived[0]

    def to_owners(array):
        return [array] + [
            lax.ppermute(array, "grp", [(a * owners_n + o, o) for o in range(owners_n)]) for a in range(1, groups)
        ]

    kept = to_owners(keep)
    others = to_owners(arrived)
    sources = kept + others

    slots = grp_size * most
    rows = call(
        functools.partial(unpack_kernel, owners_n=owners_n, most=most),
        sds((NFACES + 1, slots, NCOARSE * NCOARSE), BF16),
        [pltpu.VMEM((slots * ROW_TILES, LANES), F32), pltpu.VMEM((slots, ROW_TILES * LANES), F32)],
        where, *sources, jnp.asarray(spread_tables()),
        in_specs=[SMALL] + [VMEM] * (len(sources) + 1),
        name="unpack",
    )
    return jnp.transpose(rows, (1, 0, 2))


def solution(mesh):
    in_specs = (
        P(("slab", "grp"), None, None),
        P(("slab", "grp"), None, None),
        P(("slab", "grp"), None, None),
        P(("slab", "grp")),
        P(("slab", "grp")),
    )
    out_specs = P(("slab", "grp"), None, None)
    return jax.shard_map(shards, mesh=mesh, in_specs=in_specs, out_specs=out_specs, check_vma=False)
```

```python
import functools

import jax
import jax.numpy as jnp
import numpy as np
from jax import lax
from jax.experimental import pallas as pl
from jax.experimental.pallas import tpu as pltpu
from jax.sharding import PartitionSpec as P


NV = 5
PF = 4
PM = 2
PC = 1
LANES = 128
F32 = jnp.float32
BF16 = jnp.bfloat16
VMEM = pl.BlockSpec(memory_space=pltpu.VMEM)
SMALL = pl.BlockSpec(memory_space=pltpu.SMEM)


def gll_points(degree):
    if degree == 1:
        return np.array([-1.0, 1.0])
    if degree == 2:
        return np.array([-1.0, 0.0, 1.0])
    inner_pt = np.sqrt(3.0 / 7.0)
    return np.array([-1.0, -inner_pt, 0.0, inner_pt, 1.0])


def lagrange(source_deg, target_deg):
    source = gll_points(source_deg)
    target = gll_points(target_deg)
    result = np.ones((target_deg + 1, source_deg + 1))
    for j in range(source_deg + 1):
        for m in range(source_deg + 1):
            if m != j:
                result[:, j] = result[:, j] * (target - source[m]) / (source[j] - source[m])
    return result


def round_up(value, step):
    return -(-value // step) * step


def split(table):
    leading = table.astype(np.float32).astype(BF16)
    remainder = (table - leading.astype(np.float64)).astype(np.float32).astype(BF16)
    return leading, remainder


LINE = lagrange(PM, PF) @ lagrange(PC, PM)
SIDE = PC + 1
NCOARSE = NV * SIDE**3
PLANE = SIDE**2
UNIT = PLANE * NV * PLANE
FACE = NV * UNIT
VROW = SIDE**3 * NCOARSE
NFACES = 6
DIAG_AT = round_up(NFACES * FACE, LANES)
ROW_TILES = round_up(DIAG_AT + NCOARSE * NCOARSE, LANES) // LANES
LEFT_TILES = round_up(VROW, LANES) // LANES


def face_table():
    face = np.kron(LINE, LINE)
    table = np.kron(face, np.kron(np.eye(NV), face))
    leading, remainder = split(table)
    out = np.zeros((table.shape[0], 2 * LANES), BF16)
    out[:, :UNIT] = leading
    out[:, LANES : LANES + UNIT] = remainder
    return out


def diag_tables():
    table = np.kron(np.eye(NV), np.kron(np.kron(LINE, LINE), LINE))
    leading, remainder = split(table)
    right = np.zeros((table.shape[0], LANES), BF16)
    right[:, :NCOARSE] = leading
    right[:, LANES // 2 : LANES // 2 + NCOARSE] = remainder
    left = np.concatenate([leading.T, remainder.T], axis=0)
    return right, left


def plane_turns():
    flat = np.arange(PLANE)
    first, second = flat // SIDE, flat % SIDE
    tables = []
    for _ in range(4):
        tables.append(first * SIDE + second)
        first, second = SIDE - 1 - second, first
    return tables


def turn_tables():
    out = np.zeros((2, UNIT, 4 * LANES), BF16)
    for o, table in enumerate(plane_turns()):
        for c in range(PLANE):
            for w in range(NV):
                for d in range(PLANE):
                    new = (c * NV + w) * PLANE + d
                    out[0, (c * NV + w) * PLANE + table[d], o * LANES + new] = 1
                    out[1, (table[c] * NV + w) * PLANE + d, o * LANES + new] = 1
    return out


def spread_tables():
    half = VROW % LANES
    out = np.zeros((NFACES, UNIT, 2 * LEFT_TILES * LANES), BF16)

    def full(plane, axis, level):
        pair = [plane // SIDE, plane % SIDE]
        pair.insert(axis, level)
        return (pair[0] * SIDE + pair[1]) * SIDE + pair[2]

    for face in range(NFACES):
        axis, high = face // 2, face % 2
        for c in range(PLANE):
            for w in range(NV):
                for d in range(PLANE):
                    row = full(c, axis, high)
                    col = w * SIDE**3 + full(d, axis, 1 - high)
                    unit = (c * NV + w) * PLANE + d
                    out[face, unit, row * NCOARSE + col] = 1
                    out[face, unit, LEFT_TILES * LANES + half + row * NCOARSE + col] = 1
    return out


def face_product(pieces, pitch, table, stacked, products):
    width = table.shape[0]
    if sum(x.shape[0] for _, x in pieces) < pitch:
        stacked[...] = jnp.zeros_like(stacked)
    for v in range(NV):
        for start, x in pieces:
            at = v * pitch + start
            stacked[at : at + x.shape[0], :] = x[:, v * width : (v + 1) * width]
    y = jnp.dot(stacked[...], table[...], preferred_element_type=F32)
    products[...] = y[:, :LANES] + y[:, LANES:]


def as_column(row, count):
    shape = (count, row.shape[1])
    diagonal = lax.broadcasted_iota(jnp.int32, shape, 0) == lax.broadcasted_iota(jnp.int32, shape, 1)
    return jnp.sum(jnp.where(diagonal, row, 0), axis=1, keepdims=True)


def placement(owner, me, owners_n, most):
    elems = owner.shape[1]
    shape = (elems, elems)
    earlier = lax.broadcasted_iota(jnp.int32, shape, 0) < lax.broadcasted_iota(jnp.int32, shape, 1)
    same = as_column(owner, elems) == owner
    rank = jnp.sum(jnp.where(same & earlier, 1, 0), axis=0, keepdims=True)
    dest = lax.rem(owner - lax.rem(me, owners_n) + owners_n, owners_n) * most + rank
    slot = lax.broadcasted_iota(jnp.int32, (owners_n * most, elems), 0)
    return jnp.where(slot == dest, 1.0, 0.0).astype(BF16)


def xface_kernel(x_ref, table_ref, turn_ref, orient_ref, plus_ref, sent_ref, stacked, products, scratch):
    pitch = stacked.shape[0] // NV
    elems = pitch // 2
    face_product([(f * elems, x_ref.at[f]) for f in range(2)], pitch, table_ref, stacked, products)
    orient = as_column(orient_ref[...], elems)
    for which, out_ref in enumerate((plus_ref, sent_ref)):
        starts = [v * pitch + which * elems for v in range(NV)]
        units = [products[s : s + elems, :] for s in starts]
        mine = jnp.concatenate(units, axis=0)[:, :UNIT].astype(BF16)
        turned = jnp.dot(mine, turn_ref[which], preferred_element_type=F32)
        for v in range(NV):
            piece = turned[v * elems : (v + 1) * elems]
            total = jnp.zeros((elems, LANES), F32)
            for o in range(4):
                total = jnp.where(orient == o, piece[:, o * LANES : (o + 1) * LANES], total)
            scratch[:, v * UNIT : (v + 1) * UNIT] = total[:, :UNIT]
        out_ref[...] = scratch[...].astype(BF16)


def coarse_block(block, right, left):
    half = LANES // 2
    y = jnp.dot(block, right, preferred_element_type=F32)
    z = y + pltpu.roll(y, half, 1)
    lane = lax.broadcasted_iota(jnp.int32, z.shape, 1)
    high = z.astype(BF16).astype(F32)
    parts = jnp.where(lane < half, z, z - high).astype(BF16)
    g = jnp.dot(left, parts, preferred_element_type=F32)
    return g[:NCOARSE] + g[NCOARSE:] + pltpu.roll(g[:NCOARSE], half, 1)


def main_kernel(
    where_ref, diag_hbm, side_hbm, table_hbm, right_ref, left_ref, minus_ref, plus_ref, owner_ref,
    keep_ref, send_ref, blocks, side, table, stacked, products, coarse, rows, packed_scr, sems, *, many, owners_n,
):
    elems = blocks.shape[0]
    n_side = side.shape[0] // elems
    side_copy = pltpu.make_async_copy(side_hbm, side, sems.at[elems])
    table_copy = pltpu.make_async_copy(table_hbm, table, sems.at[elems + 1])

    def block_copy(e):
        return pltpu.make_async_copy(diag_hbm.at[e], blocks.at[e], sems.at[e])

    for e in range(many):
        block_copy(e).start()
    side_copy.start()
    table_copy.start()
    for e in range(many, elems):
        block_copy(e).start()
    rows[...] = jnp.zeros_like(rows)
    rows[:, :FACE] = minus_ref[...].astype(F32)
    rows[:, FACE : 2 * FACE] = plus_ref[...].astype(F32)

    def coarse_at(e):
        g = coarse_block(blocks[e], right_ref[...], left_ref[...])
        coarse[pl.ds(e * NCOARSE, NCOARSE), :] = g

    for e in range(many):
        block_copy(e).wait()
        coarse_at(e)
    side_copy.wait()
    table_copy.wait()
    pitch = stacked.shape[0] // NV
    face_product([(0, side)], pitch, table, stacked, products)
    for f in range(n_side):
        for v in range(NV):
            start = (2 + f) * FACE + v * UNIT
            unit = products[pl.ds(v * pitch + f, elems, stride=n_side), :]
            rows[:elems, start : start + UNIT] = unit[:, :UNIT]

    def some_blocks(step, carry):
        for i in range(many):
            block_copy(step * many + i).wait()
        for i in range(many):
            coarse_at(step * many + i)
        return carry

    lax.fori_loop(1, elems // many, some_blocks, 0)
    for c in range(NCOARSE):
        piece = coarse[pl.ds(c, elems, stride=NCOARSE), :]
        start = DIAG_AT + c * NCOARSE
        rows[:elems, start : start + NCOARSE] = piece[:, :NCOARSE]
    most = keep_ref.shape[1]
    slots = owners_n * most
    placer = placement(owner_ref[...], where_ref[0], owners_n, most)
    packed = jnp.dot(placer, rows[:elems].astype(BF16), preferred_element_type=F32)
    for j in range(ROW_TILES):
        packed_scr[pl.ds(j, slots, stride=ROW_TILES), :] = packed[:, j * LANES : (j + 1) * LANES]
    kept = most * ROW_TILES
    keep_ref[...] = packed_scr[:kept].astype(BF16).reshape(keep_ref.shape)
    send_ref[...] = packed_scr[kept:].astype(BF16).reshape(send_ref.shape)


def unpack_kernel(where_ref, *refs, owners_n, most):
    spread_ref, out_hbm, tiles, flat, out, sems = refs[-6:]
    kept = refs[: (len(refs) - 6) // 2]
    others = refs[(len(refs) - 6) // 2 : -6]
    slots = out.shape[1]
    me = where_ref[0]
    width = NCOARSE * NCOARSE
    half = LEFT_TILES * LANES

    def copy_out(block):
        return pltpu.make_async_copy(out.at[block], out_hbm.at[block], sems.at[block])

    @pl.when(me >= owners_n)
    def _():
        for block in range(NFACES + 1):
            out[block] = jnp.zeros(out.shape[1:], BF16)
            copy_out(block).start()

    @pl.when(me < owners_n)
    def _():
        step = most * ROW_TILES
        for a in range(len(kept)):
            for j in range(owners_n):
                chunk = kept[a][0] if j == 0 else others[a][j - 1]
                source = a * owners_n + lax.rem(me - j + owners_n, owners_n)
                tiles[pl.ds(source * step, step), :] = chunk.astype(F32).reshape(step, LANES)
        for j in range(ROW_TILES):
            flat[:, j * LANES : (j + 1) * LANES] = tiles[pl.ds(j, slots, stride=ROW_TILES), :]
        out[0] = flat[:, DIAG_AT : DIAG_AT + width].astype(BF16)
        copy_out(0).start()
        for f in range(NFACES):
            sums = {}
            for parity in range(2):
                vs = list(range(parity, NV, 2))
                cuts = [f * FACE + v * UNIT for v in vs]
                units = jnp.concatenate([flat[:, c : c + UNIT] for c in cuts], axis=0).astype(BF16)
                table = spread_ref[f, :, parity * half : (parity + 1) * half]
                spread = jnp.dot(units, table, preferred_element_type=F32)
                for row, v in enumerate(vs):
                    for t in range(LEFT_TILES):
                        tile = v * VROW // LANES + t
                        if tile * LANES >= width:
                            continue
                        value = spread[row * slots : (row + 1) * slots, t * LANES : (t + 1) * LANES]
                        sums[tile] = sums[tile] + value if tile in sums else value
            for tile, value in sums.items():
                cut = min(LANES, width - tile * LANES)
                out[f + 1, :, tile * LANES : tile * LANES + cut] = value[:, :cut].astype(BF16)
            copy_out(f + 1).start()

    for block in range(NFACES + 1):
        copy_out(block).wait()


def call(kernel, out_shape, scratch, *args, **kwargs):
    return pl.pallas_call(kernel, out_shape=out_shape, scratch_shapes=scratch, **kwargs)(*args)


def shards(diag_jac, xface_jac, side_jac, orient, owner):
    elems = diag_jac.shape[0]
    nf = diag_jac.shape[1]
    length = xface_jac.shape[2]
    pad = round_up(elems, 16)
    grp_size = lax.axis_size("grp")
    slab_size = lax.axis_size("slab")
    owners_n = grp_size // 4
    most = max(2, 3 * elems // (2 * owners_n))
    where = lax.axis_index("grp").astype(jnp.int32)[None]
    table = jnp.asarray(face_table())
    right, left = (jnp.asarray(t) for t in diag_tables())

    sds = jax.ShapeDtypeStruct
    width = table.shape[0]
    plus, sent = call(
        xface_kernel,
        (sds((pad, FACE), BF16), sds((pad, FACE), BF16)),
        [
            pltpu.VMEM((NV * 2 * pad, width), BF16),
            pltpu.VMEM((NV * 2 * pad, LANES), F32),
            pltpu.VMEM((pad, FACE), F32),
        ],
        jnp.transpose(xface_jac, (1, 0, 2)), table, jnp.asarray(turn_tables()), orient[None, :], name="xface",
    )
    minus = lax.ppermute(sent, "slab", [(i, (i + 1) % slab_size) for i in range(slab_size)])

    many = max(n for n in range(1, 4) if elems % n == 0)
    n_side = side_jac.shape[1]
    pitch = round_up(n_side * elems, 16)
    chunk = (most, ROW_TILES, LANES)
    keep, send = call(
        functools.partial(main_kernel, many=many, owners_n=owners_n),
        (sds((1,) + chunk, BF16), sds((owners_n - 1,) + chunk, BF16)),
        [
            pltpu.VMEM((elems, nf, nf), BF16),
            pltpu.VMEM((n_side * elems, length), BF16),
            pltpu.VMEM(table.shape, BF16),
            pltpu.VMEM((NV * pitch, width), BF16),
            pltpu.VMEM((NV * pitch, LANES), F32),
            pltpu.VMEM((elems * NCOARSE, LANES), F32),
            pltpu.VMEM((pad, ROW_TILES * LANES), F32),
            pltpu.VMEM((owners_n * most * ROW_TILES, LANES), F32),
            pltpu.SemaphoreType.DMA((elems + 2,)),
        ],
        where, diag_jac, side_jac.reshape(n_side * elems, length), table, right, left, minus, plus, owner[None, :],
        in_specs=[SMALL] + [pl.BlockSpec(memory_space=pl.ANY)] * 3 + [VMEM] * 5,
        name="main",
    )

    groups = grp_size // owners_n
    arrived = []
    for j in range(1, owners_n):
        pairs = [(a * owners_n + o, a * owners_n + (o + j) % owners_n) for a in range(groups) for o in range(owners_n)]
        arrived.append(lax.ppermute(send[j - 1 : j], "grp", pairs))
    arrived = jnp.concatenate(arrived, axis=0) if len(arrived) > 1 else arrived[0]

    def to_owners(array):
        return [array] + [
            lax.ppermute(array, "grp", [(a * owners_n + o, o) for o in range(owners_n)]) for a in range(1, groups)
        ]

    kept = to_owners(keep)
    others = to_owners(arrived)
    sources = kept + others

    slots = grp_size * most
    rows = call(
        functools.partial(unpack_kernel, owners_n=owners_n, most=most),
        sds((NFACES + 1, slots, NCOARSE * NCOARSE), BF16),
        [
            pltpu.VMEM((slots * ROW_TILES, LANES), F32),
            pltpu.VMEM((slots, ROW_TILES * LANES), F32),
            pltpu.VMEM((NFACES + 1, slots, NCOARSE * NCOARSE), BF16),
            pltpu.SemaphoreType.DMA((NFACES + 1,)),
        ],
        where, *sources, jnp.asarray(spread_tables()),
        in_specs=[SMALL] + [VMEM] * (len(sources) + 1),
        out_specs=pl.BlockSpec(memory_space=pl.ANY),
        name="unpack",
    )
    return jnp.transpose(rows, (1, 0, 2))


def solution(mesh):
    in_specs = (
        P(("slab", "grp"), None, None),
        P(("slab", "grp"), None, None),
        P(("slab", "grp"), None, None),
        P(("slab", "grp")),
        P(("slab", "grp")),
    )
    out_specs = P(("slab", "grp"), None, None)
    return jax.shard_map(shards, mesh=mesh, in_specs=in_specs, out_specs=out_specs, check_vma=False)
```

```python
import functools

import jax
import jax.numpy as jnp
import numpy as np
from jax import lax
from jax.experimental import pallas as pl
from jax.experimental.pallas import tpu as pltpu
from jax.sharding import PartitionSpec as P


NV = 5
PF = 4
PM = 2
PC = 1
LANES = 128
F32 = jnp.float32
BF16 = jnp.bfloat16
VMEM = pl.BlockSpec(memory_space=pltpu.VMEM)
SMALL = pl.BlockSpec(memory_space=pltpu.SMEM)


def gll_points(degree):
    if degree == 1:
        return np.array([-1.0, 1.0])
    if degree == 2:
        return np.array([-1.0, 0.0, 1.0])
    inner_pt = np.sqrt(3.0 / 7.0)
    return np.array([-1.0, -inner_pt, 0.0, inner_pt, 1.0])


def lagrange(source_deg, target_deg):
    source = gll_points(source_deg)
    target = gll_points(target_deg)
    result = np.ones((target_deg + 1, source_deg + 1))
    for j in range(source_deg + 1):
        for m in range(source_deg + 1):
            if m != j:
                result[:, j] = result[:, j] * (target - source[m]) / (source[j] - source[m])
    return result


def round_up(value, step):
    return -(-value // step) * step


def split(table):
    leading = table.astype(np.float32).astype(BF16)
    remainder = (table - leading.astype(np.float64)).astype(np.float32).astype(BF16)
    return leading, remainder


LINE = lagrange(PM, PF) @ lagrange(PC, PM)
SIDE = PC + 1
NCOARSE = NV * SIDE**3
PLANE = SIDE**2
UNIT = PLANE * NV * PLANE
FACE = NV * UNIT
VROW = SIDE**3 * NCOARSE
NFACES = 6
DIAG_AT = round_up(NFACES * FACE, LANES)
ROW_TILES = round_up(DIAG_AT + NCOARSE * NCOARSE, LANES) // LANES
LEFT_TILES = round_up(VROW, LANES) // LANES


def face_table():
    face = np.kron(LINE, LINE)
    table = np.kron(face, np.kron(np.eye(NV), face))
    leading, remainder = split(table)
    out = np.zeros((table.shape[0], 2 * LANES), BF16)
    out[:, :UNIT] = leading
    out[:, LANES : LANES + UNIT] = remainder
    return out


def diag_tables():
    table = np.kron(np.eye(NV), np.kron(np.kron(LINE, LINE), LINE))
    leading, remainder = split(table)
    right = np.zeros((table.shape[0], LANES), BF16)
    right[:, :NCOARSE] = leading
    right[:, LANES // 2 : LANES // 2 + NCOARSE] = remainder
    left = np.concatenate([leading.T, remainder.T], axis=0)
    return right, left


def plane_turns():
    flat = np.arange(PLANE)
    first, second = flat // SIDE, flat % SIDE
    tables = []
    for _ in range(4):
        tables.append(first * SIDE + second)
        first, second = SIDE - 1 - second, first
    return tables


def turn_tables():
    out = np.zeros((2, UNIT, 4 * LANES), BF16)
    for o, table in enumerate(plane_turns()):
        for c in range(PLANE):
            for w in range(NV):
                for d in range(PLANE):
                    new = (c * NV + w) * PLANE + d
                    out[0, (c * NV + w) * PLANE + table[d], o * LANES + new] = 1
                    out[1, (table[c] * NV + w) * PLANE + d, o * LANES + new] = 1
    return out


def spread_tables():
    half = VROW % LANES
    out = np.zeros((NFACES, UNIT, 2 * LEFT_TILES * LANES), BF16)

    def full(plane, axis, level):
        pair = [plane // SIDE, plane % SIDE]
        pair.insert(axis, level)
        return (pair[0] * SIDE + pair[1]) * SIDE + pair[2]

    for face in range(NFACES):
        axis, high = face // 2, face % 2
        for c in range(PLANE):
            for w in range(NV):
                for d in range(PLANE):
                    row = full(c, axis, high)
                    col = w * SIDE**3 + full(d, axis, 1 - high)
                    unit = (c * NV + w) * PLANE + d
                    out[face, unit, row * NCOARSE + col] = 1
                    out[face, unit, LEFT_TILES * LANES + half + row * NCOARSE + col] = 1
    return out


def face_product(pieces, pitch, table, stacked, products):
    width = table.shape[0]
    if sum(x.shape[0] for _, x in pieces) < pitch:
        stacked[...] = jnp.zeros_like(stacked)
    for v in range(NV):
        for start, x in pieces:
            at = v * pitch + start
            stacked[at : at + x.shape[0], :] = x[:, v * width : (v + 1) * width]
    y = jnp.dot(stacked[...], table[...], preferred_element_type=F32)
    products[...] = y[:, :LANES] + y[:, LANES:]


def as_column(row, count):
    shape = (count, row.shape[1])
    diagonal = lax.broadcasted_iota(jnp.int32, shape, 0) == lax.broadcasted_iota(jnp.int32, shape, 1)
    return jnp.sum(jnp.where(diagonal, row, 0), axis=1, keepdims=True)


def placement(owner, me, owners_n, most):
    elems = owner.shape[1]
    shape = (elems, elems)
    earlier = lax.broadcasted_iota(jnp.int32, shape, 0) < lax.broadcasted_iota(jnp.int32, shape, 1)
    same = as_column(owner, elems) == owner
    rank = jnp.sum(jnp.where(same & earlier, 1, 0), axis=0, keepdims=True)
    dest = lax.rem(owner - lax.rem(me, owners_n) + owners_n, owners_n) * most + rank
    slot = lax.broadcasted_iota(jnp.int32, (owners_n * most, elems), 0)
    return jnp.where(slot == dest, 1.0, 0.0).astype(BF16)


def xface_kernel(x_ref, table_ref, turn_ref, orient_ref, plus_ref, sent_ref, stacked, products, scratch):
    pitch = stacked.shape[0] // NV
    elems = pitch // 2
    face_product([(f * elems, x_ref.at[f]) for f in range(2)], pitch, table_ref, stacked, products)
    orient = as_column(orient_ref[...], elems)
    for which, out_ref in enumerate((plus_ref, sent_ref)):
        starts = [v * pitch + which * elems for v in range(NV)]
        units = [products[s : s + elems, :] for s in starts]
        mine = jnp.concatenate(units, axis=0)[:, :UNIT].astype(BF16)
        turned = jnp.dot(mine, turn_ref[which], preferred_element_type=F32)
        for v in range(NV):
            piece = turned[v * elems : (v + 1) * elems]
            total = jnp.zeros((elems, LANES), F32)
            for o in range(4):
                total = jnp.where(orient == o, piece[:, o * LANES : (o + 1) * LANES], total)
            scratch[:, v * UNIT : (v + 1) * UNIT] = total[:, :UNIT]
        out_ref[...] = scratch[...].astype(BF16)


def coarse_block(block, right, left):
    w = jnp.dot(left, block, preferred_element_type=F32)
    w = w[:NCOARSE] + w[NCOARSE:]
    rest = w - w.astype(BF16).astype(F32)
    g = jnp.dot(jnp.concatenate([w, rest], axis=0).astype(BF16), right, preferred_element_type=F32)
    return g[:NCOARSE] + g[NCOARSE:] + pltpu.roll(g[:NCOARSE], LANES // 2, 1)


def main_kernel(
    diag_hbm, side_hbm, table_hbm, right_ref, left_ref, out_ref,
    blocks, side, table, stacked, products, coarse, rows, sems, *, many,
):
    elems = blocks.shape[0]
    n_side = side.shape[0] // elems
    side_copy = pltpu.make_async_copy(side_hbm, side, sems.at[elems])
    table_copy = pltpu.make_async_copy(table_hbm, table, sems.at[elems + 1])

    def block_copy(e):
        return pltpu.make_async_copy(diag_hbm.at[e], blocks.at[e], sems.at[e])

    side_copy.start()
    table_copy.start()
    for e in range(elems):
        block_copy(e).start()
    rows[...] = jnp.zeros_like(rows)
    side_copy.wait()
    table_copy.wait()
    pitch = stacked.shape[0] // NV
    face_product([(0, side)], pitch, table, stacked, products)
    for f in range(n_side):
        for v in range(NV):
            start = (2 + f) * FACE + v * UNIT
            unit = products[pl.ds(v * pitch + f, elems, stride=n_side), :]
            rows[:elems, start : start + UNIT] = unit[:, :UNIT]

    def some_blocks(step, carry):
        for i in range(many):
            block_copy(step * many + i).wait()
        for i in range(many):
            e = step * many + i
            g = coarse_block(blocks[e], right_ref[...], left_ref[...])
            coarse[pl.ds(e * NCOARSE, NCOARSE), :] = g
        return carry

    lax.fori_loop(0, elems // many, some_blocks, 0)
    for c in range(NCOARSE):
        piece = coarse[pl.ds(c, elems, stride=NCOARSE), :]
        start = DIAG_AT + c * NCOARSE
        rows[:elems, start : start + NCOARSE] = piece[:, :NCOARSE]
    out_ref[...] = rows[...].astype(BF16)


def pack_kernel(where_ref, rows_ref, minus_ref, plus_ref, owner_ref, keep_ref, send_ref, head, packed_scr, *, owners_n):
    elems = owner_ref.shape[1]
    cut = head.shape[1]
    head[...] = rows_ref[:, :cut].astype(F32)
    head[:, :FACE] = minus_ref[...].astype(F32)
    head[:, FACE : 2 * FACE] = plus_ref[...].astype(F32)
    most = keep_ref.shape[1]
    slots = owners_n * most
    placer = placement(owner_ref[...], where_ref[0], owners_n, most)
    first = jnp.dot(placer, head[:elems].astype(BF16), preferred_element_type=F32)
    rest = jnp.dot(placer, rows_ref[:elems, cut:], preferred_element_type=F32)
    for j in range(ROW_TILES):
        source, at = (first, j * LANES) if j * LANES < cut else (rest, j * LANES - cut)
        packed_scr[pl.ds(j, slots, stride=ROW_TILES), :] = source[:, at : at + LANES]
    kept = most * ROW_TILES
    keep_ref[...] = packed_scr[:kept].astype(BF16).reshape(keep_ref.shape)
    send_ref[...] = packed_scr[kept:].astype(BF16).reshape(send_ref.shape)


def unpack_kernel(where_ref, *refs, owners_n, most):
    spread_ref, out_hbm, tiles, flat, out, sems = refs[-6:]
    kept = refs[: (len(refs) - 6) // 2]
    others = refs[(len(refs) - 6) // 2 : -6]
    slots = out.shape[1]
    me = where_ref[0]
    width = NCOARSE * NCOARSE
    half = LEFT_TILES * LANES

    def copy_out(block):
        return pltpu.make_async_copy(out.at[block], out_hbm.at[block], sems.at[block])

    @pl.when(me >= owners_n)
    def _():
        for block in range(NFACES + 1):
            out[block] = jnp.zeros(out.shape[1:], BF16)
            copy_out(block).start()

    @pl.when(me < owners_n)
    def _():
        step = most * ROW_TILES
        for a in range(len(kept)):
            for j in range(owners_n):
                chunk = kept[a][0] if j == 0 else others[a][j - 1]
                source = a * owners_n + lax.rem(me - j + owners_n, owners_n)
                tiles[pl.ds(source * step, step), :] = chunk.astype(F32).reshape(step, LANES)
        for j in range(ROW_TILES):
            flat[:, j * LANES : (j + 1) * LANES] = tiles[pl.ds(j, slots, stride=ROW_TILES), :]
        out[0] = flat[:, DIAG_AT : DIAG_AT + width].astype(BF16)
        copy_out(0).start()
        for f in range(NFACES):
            sums = {}
            for parity in range(2):
                vs = list(range(parity, NV, 2))
                cuts = [f * FACE + v * UNIT for v in vs]
                units = jnp.concatenate([flat[:, c : c + UNIT] for c in cuts], axis=0).astype(BF16)
                table = spread_ref[f, :, parity * half : (parity + 1) * half]
                spread = jnp.dot(units, table, preferred_element_type=F32)
                for row, v in enumerate(vs):
                    for t in range(LEFT_TILES):
                        tile = v * VROW // LANES + t
                        if tile * LANES >= width:
                            continue
                        value = spread[row * slots : (row + 1) * slots, t * LANES : (t + 1) * LANES]
                        sums[tile] = sums[tile] + value if tile in sums else value
            for tile, value in sums.items():
                cut = min(LANES, width - tile * LANES)
                out[f + 1, :, tile * LANES : tile * LANES + cut] = value[:, :cut].astype(BF16)
            copy_out(f + 1).start()

    for block in range(NFACES + 1):
        copy_out(block).wait()


def call(kernel, out_shape, scratch, *args, **kwargs):
    return pl.pallas_call(kernel, out_shape=out_shape, scratch_shapes=scratch, **kwargs)(*args)


def shards(diag_jac, xface_jac, side_jac, orient, owner):
    elems = diag_jac.shape[0]
    nf = diag_jac.shape[1]
    length = xface_jac.shape[2]
    pad = round_up(elems, 16)
    grp_size = lax.axis_size("grp")
    slab_size = lax.axis_size("slab")
    owners_n = grp_size // 4
    most = max(2, 3 * elems // (2 * owners_n))
    where = lax.axis_index("grp").astype(jnp.int32)[None]
    table = jnp.asarray(face_table())
    right, left = (jnp.asarray(t) for t in diag_tables())

    sds = jax.ShapeDtypeStruct
    width = table.shape[0]
    plus, sent = call(
        xface_kernel,
        (sds((pad, FACE), BF16), sds((pad, FACE), BF16)),
        [
            pltpu.VMEM((NV * 2 * pad, width), BF16),
            pltpu.VMEM((NV * 2 * pad, LANES), F32),
            pltpu.VMEM((pad, FACE), F32),
        ],
        jnp.transpose(xface_jac, (1, 0, 2)), table, jnp.asarray(turn_tables()), orient[None, :], name="xface",
    )
    minus = lax.ppermute(sent, "slab", [(i, (i + 1) % slab_size) for i in range(slab_size)])

    many = max(n for n in range(1, 4) if elems % n == 0)
    n_side = side_jac.shape[1]
    pitch = round_up(n_side * elems, 16)
    chunk = (most, ROW_TILES, LANES)
    rows = call(
        functools.partial(main_kernel, many=many),
        sds((pad, ROW_TILES * LANES), BF16),
        [
            pltpu.VMEM((elems, nf, nf), BF16),
            pltpu.VMEM((n_side * elems, length), BF16),
            pltpu.VMEM(table.shape, BF16),
            pltpu.VMEM((NV * pitch, width), BF16),
            pltpu.VMEM((NV * pitch, LANES), F32),
            pltpu.VMEM((elems * NCOARSE, LANES), F32),
            pltpu.VMEM((pad, ROW_TILES * LANES), F32),
            pltpu.SemaphoreType.DMA((elems + 2,)),
        ],
        diag_jac, side_jac.reshape(n_side * elems, length), table, right, left,
        in_specs=[pl.BlockSpec(memory_space=pl.ANY)] * 3 + [VMEM] * 2,
        name="main",
    )
    keep, send = call(
        functools.partial(pack_kernel, owners_n=owners_n),
        (sds((1,) + chunk, BF16), sds((owners_n - 1,) + chunk, BF16)),
        [
            pltpu.VMEM((pad, round_up(2 * FACE, LANES)), F32),
            pltpu.VMEM((owners_n * most * ROW_TILES, LANES), F32),
        ],
        where, rows, minus, plus, owner[None, :],
        in_specs=[SMALL] + [VMEM] * 4,
        name="pack",
    )

    groups = grp_size // owners_n
    arrived = []
    for j in range(1, owners_n):
        pairs = [(a * owners_n + o, a * owners_n + (o + j) % owners_n) for a in range(groups) for o in range(owners_n)]
        arrived.append(lax.ppermute(send[j - 1 : j], "grp", pairs))
    arrived = jnp.concatenate(arrived, axis=0) if len(arrived) > 1 else arrived[0]

    def to_owners(array):
        return [array] + [
            lax.ppermute(array, "grp", [(a * owners_n + o, o) for o in range(owners_n)]) for a in range(1, groups)
        ]

    kept = to_owners(keep)
    others = to_owners(arrived)
    sources = kept + others

    slots = grp_size * most
    rows = call(
        functools.partial(unpack_kernel, owners_n=owners_n, most=most),
        sds((NFACES + 1, slots, NCOARSE * NCOARSE), BF16),
        [
            pltpu.VMEM((slots * ROW_TILES, LANES), F32),
            pltpu.VMEM((slots, ROW_TILES * LANES), F32),
            pltpu.VMEM((NFACES + 1, slots, NCOARSE * NCOARSE), BF16),
            pltpu.SemaphoreType.DMA((NFACES + 1,)),
        ],
        where, *sources, jnp.asarray(spread_tables()),
        in_specs=[SMALL] + [VMEM] * (len(sources) + 1),
        out_specs=pl.BlockSpec(memory_space=pl.ANY),
        name="unpack",
    )
    return jnp.transpose(rows, (1, 0, 2))


def solution(mesh):
    in_specs = (
        P(("slab", "grp"), None, None),
        P(("slab", "grp"), None, None),
        P(("slab", "grp"), None, None),
        P(("slab", "grp")),
        P(("slab", "grp")),
    )
    out_specs = P(("slab", "grp"), None, None)
    return jax.shard_map(shards, mesh=mesh, in_specs=in_specs, out_specs=out_specs, check_vma=False)
```

```python
import functools

import jax
import jax.numpy as jnp
import numpy as np
from jax import lax
from jax.experimental import pallas as pl
from jax.experimental.pallas import tpu as pltpu
from jax.sharding import PartitionSpec as P


NV = 5
PF = 4
PM = 2
PC = 1
LANES = 128
GROUPS = 4
F32 = jnp.float32
BF16 = jnp.bfloat16
VMEM = pl.BlockSpec(memory_space=pltpu.VMEM)
SMALL = pl.BlockSpec(memory_space=pltpu.SMEM)


def gll_points(degree):
    if degree == 1:
        return np.array([-1.0, 1.0])
    if degree == 2:
        return np.array([-1.0, 0.0, 1.0])
    inner_pt = np.sqrt(3.0 / 7.0)
    return np.array([-1.0, -inner_pt, 0.0, inner_pt, 1.0])


def lagrange(source_deg, target_deg):
    source = gll_points(source_deg)
    target = gll_points(target_deg)
    result = np.ones((target_deg + 1, source_deg + 1))
    for j in range(source_deg + 1):
        for m in range(source_deg + 1):
            if m != j:
                result[:, j] = result[:, j] * (target - source[m]) / (source[j] - source[m])
    return result


def round_up(value, step):
    return -(-value // step) * step


def split(table):
    leading = table.astype(np.float32).astype(BF16)
    remainder = (table - leading.astype(np.float64)).astype(np.float32).astype(BF16)
    return leading, remainder


LINE = lagrange(PM, PF) @ lagrange(PC, PM)
SIDE = PC + 1
NCOARSE = NV * SIDE**3
PLANE = SIDE**2
UNIT = PLANE * NV * PLANE
FACE = NV * UNIT
VROW = SIDE**3 * NCOARSE
NFACES = 6
DIAG_AT = round_up(NFACES * FACE, LANES)
ROW_TILES = round_up(DIAG_AT + NCOARSE * NCOARSE, LANES) // LANES
LEFT_TILES = round_up(VROW, LANES) // LANES


def face_table():
    face = np.kron(LINE, LINE)
    table = np.kron(face, np.kron(np.eye(NV), face))
    leading, remainder = split(table)
    return np.concatenate([leading.T, remainder.T], axis=0)


def diag_tables():
    table = np.kron(np.eye(NV), np.kron(np.kron(LINE, LINE), LINE))
    leading, remainder = split(table)
    right = np.zeros((table.shape[0], LANES), BF16)
    right[:, :NCOARSE] = leading
    right[:, LANES // 2 : LANES // 2 + NCOARSE] = remainder
    left = np.concatenate([leading.T, remainder.T], axis=0)
    return right, left


def plane_turns():
    flat = np.arange(PLANE)
    first, second = flat // SIDE, flat % SIDE
    tables = []
    for _ in range(4):
        tables.append(first * SIDE + second)
        first, second = SIDE - 1 - second, first
    return tables


def turn_tables():
    out = np.zeros((2, UNIT, 4 * LANES), BF16)
    for o, table in enumerate(plane_turns()):
        for c in range(PLANE):
            for w in range(NV):
                for d in range(PLANE):
                    new = (c * NV + w) * PLANE + d
                    out[0, (c * NV + w) * PLANE + table[d], o * LANES + new] = 1
                    out[1, (table[c] * NV + w) * PLANE + d, o * LANES + new] = 1
    return out


def spread_tables():
    half = VROW % LANES
    out = np.zeros((NFACES, UNIT, 2 * LEFT_TILES * LANES), BF16)

    def full(plane, axis, level):
        pair = [plane // SIDE, plane % SIDE]
        pair.insert(axis, level)
        return (pair[0] * SIDE + pair[1]) * SIDE + pair[2]

    for face in range(NFACES):
        axis, high = face // 2, face % 2
        for c in range(PLANE):
            for w in range(NV):
                for d in range(PLANE):
                    row = full(c, axis, high)
                    col = w * SIDE**3 + full(d, axis, 1 - high)
                    unit = (c * NV + w) * PLANE + d
                    out[face, unit, row * NCOARSE + col] = 1
                    out[face, unit, LEFT_TILES * LANES + half + row * NCOARSE + col] = 1
    return out


def face_product(pieces, pitch, table, stacked, products):
    width = table.shape[1]
    if sum(x.shape[0] for _, x in pieces) < pitch:
        stacked[...] = jnp.zeros_like(stacked)
    for v in range(NV):
        for start, x in pieces:
            at = v * pitch + start
            stacked[at : at + x.shape[0], :] = x[:, v * width : (v + 1) * width]
    y = lax.dot_general(stacked[...], table[...], (((1,), (1,)), ((), ())), preferred_element_type=F32)
    products[:, :UNIT] = y[:, :UNIT] + y[:, UNIT:]


def as_column(row, count):
    shape = (count, row.shape[1])
    diagonal = lax.broadcasted_iota(jnp.int32, shape, 0) == lax.broadcasted_iota(jnp.int32, shape, 1)
    return jnp.sum(jnp.where(diagonal, row, 0), axis=1, keepdims=True)


def placement(owner, me, owners_n, most):
    elems = owner.shape[1]
    shape = (elems, elems)
    earlier = lax.broadcasted_iota(jnp.int32, shape, 0) < lax.broadcasted_iota(jnp.int32, shape, 1)
    same = as_column(owner, elems) == owner
    rank = jnp.sum(jnp.where(same & earlier, 1, 0), axis=0, keepdims=True)
    dest = lax.rem(owner - lax.rem(me, owners_n) + owners_n, owners_n) * most + rank
    slot = lax.broadcasted_iota(jnp.int32, (owners_n * most, elems), 0)
    return jnp.where(slot == dest, 1.0, 0.0).astype(BF16)


def faces_kernel(
    x_hbm, side_hbm, table_hbm, turn_ref, orient_ref, plus_ref, sent_ref, out_ref,
    x, side, table, x_stacked, x_products, stacked, products, scratch, rows, sems,
):
    copies = [
        pltpu.make_async_copy(source, target, sems.at[i])
        for i, (source, target) in enumerate([(table_hbm, table), (x_hbm, x), (side_hbm, side)])
    ]
    for copy in copies:
        copy.start()
    x_pitch = x_stacked.shape[0] // NV
    pad = x_pitch // 2
    orient = as_column(orient_ref[...], pad)
    copies[0].wait()
    copies[1].wait()
    face_product([(f * pad, x.at[f]) for f in range(2)], x_pitch, table, x_stacked, x_products)
    for which, turned_ref in enumerate((plus_ref, sent_ref)):
        starts = [v * x_pitch + which * pad for v in range(NV)]
        units = [x_products[s : s + pad, :] for s in starts]
        mine = jnp.concatenate(units, axis=0)[:, :UNIT].astype(BF16)
        turned = jnp.dot(mine, turn_ref[which], preferred_element_type=F32)
        for v in range(NV):
            piece = turned[v * pad : (v + 1) * pad]
            total = jnp.zeros((pad, LANES), F32)
            for o in range(4):
                total = jnp.where(orient == o, piece[:, o * LANES : (o + 1) * LANES], total)
            scratch[:, v * UNIT : (v + 1) * UNIT] = total[:, :UNIT]
        turned_ref[...] = scratch[...].astype(BF16)
    rows[...] = jnp.zeros_like(rows)
    copies[2].wait()
    elems = x.shape[1]
    n_side = side.shape[0] // elems
    pitch = stacked.shape[0] // NV
    face_product([(0, side)], pitch, table, stacked, products)
    for f in range(n_side):
        for v in range(NV):
            start = f * FACE + v * UNIT
            unit = products[pl.ds(v * pitch + f, elems, stride=n_side), :]
            rows[:elems, start : start + UNIT] = unit[:, :UNIT]
    out_ref[...] = rows[...].astype(BF16)


def coarse_block(block, right, left):
    w = jnp.dot(left, block, preferred_element_type=F32)
    w = w[:NCOARSE] + w[NCOARSE:]
    rest = w - w.astype(BF16).astype(F32)
    g = jnp.dot(jnp.concatenate([w, rest], axis=0).astype(BF16), right, preferred_element_type=F32)
    return g[:NCOARSE] + g[NCOARSE:] + pltpu.roll(g[:NCOARSE], LANES // 2, 1)


def diag_kernel(diag_hbm, right_ref, left_ref, out_ref, blocks, coarse, rows, sems, *, many):
    elems = blocks.shape[0]

    def block_copy(e):
        return pltpu.make_async_copy(diag_hbm.at[e], blocks.at[e], sems.at[e])

    for e in range(elems):
        block_copy(e).start()
    rows[...] = jnp.zeros_like(rows)

    def some_blocks(step, carry):
        for i in range(many):
            block_copy(step * many + i).wait()
        for i in range(many):
            e = step * many + i
            g = coarse_block(blocks[e], right_ref[...], left_ref[...])
            coarse[pl.ds(e * NCOARSE, NCOARSE), :] = g
        return carry

    lax.fori_loop(0, elems // many, some_blocks, 0)
    for c in range(NCOARSE):
        piece = coarse[pl.ds(c, elems, stride=NCOARSE), :]
        rows[:elems, c * NCOARSE : (c + 1) * NCOARSE] = piece[:, :NCOARSE]
    out_ref[...] = rows[...].astype(BF16)


def pack_kernel(
    where_ref, minus_ref, plus_ref, side_ref, diag_ref, owner_ref, keep_ref, send_ref, rows, packed_scr, *, owners_n,
):
    elems = owner_ref.shape[1]
    rows[...] = jnp.zeros_like(rows)
    start = 0
    for ref in (minus_ref, plus_ref, side_ref):
        rows[:, start : start + ref.shape[1]] = ref[...].astype(F32)
        start += ref.shape[1]
    rows[:, DIAG_AT : DIAG_AT + diag_ref.shape[1]] = diag_ref[...].astype(F32)
    most = keep_ref.shape[1]
    slots = owners_n * most
    placer = placement(owner_ref[...], where_ref[0], owners_n, most)
    packed = jnp.dot(placer, rows[:elems].astype(BF16), preferred_element_type=F32)
    for j in range(ROW_TILES):
        packed_scr[pl.ds(j, slots, stride=ROW_TILES), :] = packed[:, j * LANES : (j + 1) * LANES]
    kept = most * ROW_TILES
    keep_ref[...] = packed_scr[:kept].astype(BF16).reshape(keep_ref.shape)
    send_ref[...] = packed_scr[kept:].astype(BF16).reshape(send_ref.shape)


def unpack_kernel(where_ref, *refs, owners_n, most):
    spread_ref, out_hbm, tiles, flat, out, sems = refs[-6:]
    kept = refs[: (len(refs) - 6) // 2]
    others = refs[(len(refs) - 6) // 2 : -6]
    slots = out.shape[1]
    me = where_ref[0]
    width = NCOARSE * NCOARSE
    half = LEFT_TILES * LANES

    def copy_out(block):
        return pltpu.make_async_copy(out.at[block], out_hbm.at[block], sems.at[block])

    @pl.when(me >= owners_n)
    def _():
        for block in range(NFACES + 1):
            out[block] = jnp.zeros(out.shape[1:], BF16)
            copy_out(block).start()

    @pl.when(me < owners_n)
    def _():
        step = most * ROW_TILES
        for a in range(len(kept)):
            for j in range(owners_n):
                chunk = kept[a][0] if j == 0 else others[a][j - 1]
                source = a * owners_n + lax.rem(me - j + owners_n, owners_n)
                tiles[pl.ds(source * step, step), :] = chunk.astype(F32).reshape(step, LANES)
        for j in range(ROW_TILES):
            flat[:, j * LANES : (j + 1) * LANES] = tiles[pl.ds(j, slots, stride=ROW_TILES), :]
        out[0] = flat[:, DIAG_AT : DIAG_AT + width].astype(BF16)
        copy_out(0).start()
        for f in range(NFACES):
            sums = {}
            for parity in range(2):
                vs = list(range(parity, NV, 2))
                cuts = [f * FACE + v * UNIT for v in vs]
                units = jnp.concatenate([flat[:, c : c + UNIT] for c in cuts], axis=0).astype(BF16)
                table = spread_ref[f, :, parity * half : (parity + 1) * half]
                spread = jnp.dot(units, table, preferred_element_type=F32)
                for row, v in enumerate(vs):
                    for t in range(LEFT_TILES):
                        tile = v * VROW // LANES + t
                        if tile * LANES >= width:
                            continue
                        value = spread[row * slots : (row + 1) * slots, t * LANES : (t + 1) * LANES]
                        sums[tile] = sums[tile] + value if tile in sums else value
            for tile, value in sums.items():
                cut = min(LANES, width - tile * LANES)
                out[f + 1, :, tile * LANES : tile * LANES + cut] = value[:, :cut].astype(BF16)
            copy_out(f + 1).start()

    for block in range(NFACES + 1):
        copy_out(block).wait()


def call(kernel, out_shape, scratch, *args, **kwargs):
    return pl.pallas_call(kernel, out_shape=out_shape, scratch_shapes=scratch, **kwargs)(*args)


def shards(diag_jac, xface_jac, side_jac, orient, owner):
    elems = diag_jac.shape[0]
    nf = diag_jac.shape[1]
    length = xface_jac.shape[2]
    pad = round_up(elems, 16)
    grp_size = lax.axis_size("grp")
    slab_size = lax.axis_size("slab")
    owners_n = grp_size // GROUPS
    most = max(2, 3 * elems // (2 * owners_n))
    where = lax.axis_index("grp").astype(jnp.int32)[None]
    table = jnp.asarray(face_table())
    right, left = (jnp.asarray(t) for t in diag_tables())

    sds = jax.ShapeDtypeStruct
    width = table.shape[1]
    many = max(n for n in range(1, 4) if elems % n == 0)
    n_side = side_jac.shape[1]
    pitch = round_up(n_side * elems, 16)
    hbm = pl.BlockSpec(memory_space=pl.ANY)
    plus, sent, side = call(
        faces_kernel,
        (sds((pad, FACE), BF16), sds((pad, FACE), BF16), sds((pad, n_side * FACE), BF16)),
        [
            pltpu.VMEM((2, elems, length), BF16),
            pltpu.VMEM((n_side * elems, length), BF16),
            pltpu.VMEM(table.shape, BF16),
            pltpu.VMEM((NV * 2 * pad, width), BF16),
            pltpu.VMEM((NV * 2 * pad, LANES), F32),
            pltpu.VMEM((NV * pitch, width), BF16),
            pltpu.VMEM((NV * pitch, LANES), F32),
            pltpu.VMEM((pad, FACE), F32),
            pltpu.VMEM((pad, n_side * FACE), F32),
            pltpu.SemaphoreType.DMA((3,)),
        ],
        jnp.transpose(xface_jac, (1, 0, 2)), side_jac.reshape(n_side * elems, length), table,
        jnp.asarray(turn_tables()), orient[None, :],
        in_specs=[hbm] * 3 + [VMEM] * 2,
        name="faces",
    )
    minus = lax.ppermute(sent, "slab", [(i, (i + 1) % slab_size) for i in range(slab_size)])
    diag = call(
        functools.partial(diag_kernel, many=many),
        sds((pad, NCOARSE * NCOARSE), BF16),
        [
            pltpu.VMEM((elems, nf, nf), BF16),
            pltpu.VMEM((elems * NCOARSE, LANES), F32),
            pltpu.VMEM((pad, NCOARSE * NCOARSE), F32),
            pltpu.SemaphoreType.DMA((elems,)),
        ],
        diag_jac, right, left,
        in_specs=[hbm] + [VMEM] * 2,
        name="diag",
    )
    chunk = (most, ROW_TILES, LANES)
    keep, send = call(
        functools.partial(pack_kernel, owners_n=owners_n),
        (sds((1,) + chunk, BF16), sds((owners_n - 1,) + chunk, BF16)),
        [
            pltpu.VMEM((pad, ROW_TILES * LANES), F32),
            pltpu.VMEM((owners_n * most * ROW_TILES, LANES), F32),
        ],
        where, minus, plus, side, diag, owner[None, :],
        in_specs=[SMALL] + [VMEM] * 5,
        name="pack",
    )

    groups = grp_size // owners_n
    arrived = []
    for j in range(1, owners_n):
        pairs = [(a * owners_n + o, a * owners_n + (o + j) % owners_n) for a in range(groups) for o in range(owners_n)]
        arrived.append(lax.ppermute(send[j - 1 : j], "grp", pairs))
    arrived = jnp.concatenate(arrived, axis=0) if len(arrived) > 1 else arrived[0]

    def to_owners(array):
        results = [array]
        for a in range(1, groups):
            pairs = [(a * owners_n + o, o) for o in range(owners_n)]
            results.append(lax.ppermute(array, "grp", pairs))
        return results

    kept = to_owners(keep)
    others = to_owners(arrived)
    sources = kept + others

    slots = grp_size * most
    rows = call(
        functools.partial(unpack_kernel, owners_n=owners_n, most=most),
        sds((NFACES + 1, slots, NCOARSE * NCOARSE), BF16),
        [
            pltpu.VMEM((slots * ROW_TILES, LANES), F32),
            pltpu.VMEM((slots, ROW_TILES * LANES), F32),
            pltpu.VMEM((NFACES + 1, slots, NCOARSE * NCOARSE), BF16),
            pltpu.SemaphoreType.DMA((NFACES + 1,)),
        ],
        where, *sources, jnp.asarray(spread_tables()),
        in_specs=[SMALL] + [VMEM] * (len(sources) + 1),
        out_specs=pl.BlockSpec(memory_space=pl.ANY),
        name="unpack",
    )
    return jnp.transpose(rows, (1, 0, 2))


def solution(mesh):
    in_specs = (
        P(("slab", "grp"), None, None),
        P(("slab", "grp"), None, None),
        P(("slab", "grp"), None, None),
        P(("slab", "grp")),
        P(("slab", "grp")),
    )
    out_specs = P(("slab", "grp"), None, None)
    return jax.shard_map(shards, mesh=mesh, in_specs=in_specs, out_specs=out_specs, check_vma=False)
```

```python
import functools

import jax
import jax.numpy as jnp
import numpy as np
from jax import lax
from jax.experimental import pallas as pl
from jax.experimental.pallas import tpu as pltpu
from jax.sharding import PartitionSpec as P


NV = 5
PF = 4
PM = 2
PC = 1
LANES = 128
GROUPS = 4
F32 = jnp.float32
BF16 = jnp.bfloat16
VMEM = pl.BlockSpec(memory_space=pltpu.VMEM)
SMALL = pl.BlockSpec(memory_space=pltpu.SMEM)


def gll_points(degree):
    if degree == 1:
        return np.array([-1.0, 1.0])
    if degree == 2:
        return np.array([-1.0, 0.0, 1.0])
    inner_pt = np.sqrt(3.0 / 7.0)
    return np.array([-1.0, -inner_pt, 0.0, inner_pt, 1.0])


def lagrange(source_deg, target_deg):
    source = gll_points(source_deg)
    target = gll_points(target_deg)
    result = np.ones((target_deg + 1, source_deg + 1))
    for j in range(source_deg + 1):
        for m in range(source_deg + 1):
            if m != j:
                result[:, j] = result[:, j] * (target - source[m]) / (source[j] - source[m])
    return result


def round_up(value, step):
    return -(-value // step) * step


def split(table):
    leading = table.astype(np.float32).astype(BF16)
    remainder = (table - leading.astype(np.float64)).astype(np.float32).astype(BF16)
    return leading, remainder


LINE = lagrange(PM, PF) @ lagrange(PC, PM)
SIDE = PC + 1
NCOARSE = NV * SIDE**3
PLANE = SIDE**2
UNIT = PLANE * NV * PLANE
FACE = NV * UNIT
VROW = SIDE**3 * NCOARSE
NFACES = 6
DIAG_AT = round_up(NFACES * FACE, LANES)
ROW_TILES = round_up(DIAG_AT + NCOARSE * NCOARSE, LANES) // LANES
LEFT_TILES = round_up(VROW, LANES) // LANES


def face_table():
    face = np.kron(LINE, LINE)
    table = np.kron(face, np.kron(np.eye(NV), face))
    leading, remainder = split(table)
    return np.concatenate([leading.T, remainder.T], axis=0)


def diag_tables():
    table = np.kron(np.eye(NV), np.kron(np.kron(LINE, LINE), LINE))
    leading, remainder = split(table)
    right = np.zeros((table.shape[0], LANES), BF16)
    right[:, :NCOARSE] = leading
    right[:, LANES // 2 : LANES // 2 + NCOARSE] = remainder
    left = np.concatenate([leading.T, remainder.T], axis=0)
    return right, left


def plane_turns():
    flat = np.arange(PLANE)
    first, second = flat // SIDE, flat % SIDE
    tables = []
    for _ in range(4):
        tables.append(first * SIDE + second)
        first, second = SIDE - 1 - second, first
    return tables


def turn_tables():
    out = np.zeros((2, UNIT, 4 * LANES), BF16)
    for o, table in enumerate(plane_turns()):
        for c in range(PLANE):
            for w in range(NV):
                for d in range(PLANE):
                    new = (c * NV + w) * PLANE + d
                    out[0, (c * NV + w) * PLANE + table[d], o * LANES + new] = 1
                    out[1, (table[c] * NV + w) * PLANE + d, o * LANES + new] = 1
    return out


def spread_tables():
    half = VROW % LANES
    out = np.zeros((NFACES, UNIT, 2 * LEFT_TILES * LANES), BF16)

    def full(plane, axis, level):
        pair = [plane // SIDE, plane % SIDE]
        pair.insert(axis, level)
        return (pair[0] * SIDE + pair[1]) * SIDE + pair[2]

    for face in range(NFACES):
        axis, high = face // 2, face % 2
        for c in range(PLANE):
            for w in range(NV):
                for d in range(PLANE):
                    row = full(c, axis, high)
                    col = w * SIDE**3 + full(d, axis, 1 - high)
                    unit = (c * NV + w) * PLANE + d
                    out[face, unit, row * NCOARSE + col] = 1
                    out[face, unit, LEFT_TILES * LANES + half + row * NCOARSE + col] = 1
    return out


def face_product(pieces, pitch, table, stacked, products):
    width = table.shape[1]
    if sum(x.shape[0] for _, x in pieces) < pitch:
        stacked[...] = jnp.zeros_like(stacked)
    for v in range(NV):
        for start, x in pieces:
            at = v * pitch + start
            stacked[at : at + x.shape[0], :] = x[:, v * width : (v + 1) * width]
    y = lax.dot_general(stacked[...], table[...], (((1,), (1,)), ((), ())), preferred_element_type=F32)
    products[:, :UNIT] = y[:, :UNIT] + y[:, UNIT:]


def as_column(row, count):
    shape = (count, row.shape[1])
    diagonal = lax.broadcasted_iota(jnp.int32, shape, 0) == lax.broadcasted_iota(jnp.int32, shape, 1)
    return jnp.sum(jnp.where(diagonal, row, 0), axis=1, keepdims=True)


def placement(owner, me, owners_n, most):
    elems = owner.shape[1]
    shape = (elems, elems)
    earlier = lax.broadcasted_iota(jnp.int32, shape, 0) < lax.broadcasted_iota(jnp.int32, shape, 1)
    same = as_column(owner, elems) == owner
    rank = jnp.sum(jnp.where(same & earlier, 1, 0), axis=0, keepdims=True)
    dest = lax.rem(owner - lax.rem(me, owners_n) + owners_n, owners_n) * most + rank
    slot = lax.broadcasted_iota(jnp.int32, (owners_n * most, elems), 0)
    return jnp.where(slot == dest, 1.0, 0.0).astype(BF16)


def xface_kernel(x_ref, table_ref, turn_ref, orient_ref, plus_ref, sent_ref, stacked, products, scratch):
    pitch = stacked.shape[0] // NV
    elems = pitch // 2
    face_product([(f * elems, x_ref.at[f]) for f in range(2)], pitch, table_ref, stacked, products)
    orient = as_column(orient_ref[...], elems)
    for which, out_ref in enumerate((plus_ref, sent_ref)):
        starts = [v * pitch + which * elems for v in range(NV)]
        units = [products[s : s + elems, :] for s in starts]
        mine = jnp.concatenate(units, axis=0)[:, :UNIT].astype(BF16)
        turned = jnp.dot(mine, turn_ref[which], preferred_element_type=F32)
        for v in range(NV):
            piece = turned[v * elems : (v + 1) * elems]
            total = jnp.zeros((elems, LANES), F32)
            for o in range(4):
                total = jnp.where(orient == o, piece[:, o * LANES : (o + 1) * LANES], total)
            scratch[:, v * UNIT : (v + 1) * UNIT] = total[:, :UNIT]
        out_ref[...] = scratch[...].astype(BF16)


def coarse_block(block, right, left):
    w = jnp.dot(left, block, preferred_element_type=F32)
    w = w[:NCOARSE] + w[NCOARSE:]
    rest = w - w.astype(BF16).astype(F32)
    g = jnp.dot(jnp.concatenate([w, rest], axis=0).astype(BF16), right, preferred_element_type=F32)
    return g[:NCOARSE] + g[NCOARSE:] + pltpu.roll(g[:NCOARSE], LANES // 2, 1)


def main_kernel(
    diag_hbm, side_hbm, table_hbm, right_ref, left_ref, out_ref,
    blocks, side, table, stacked, products, coarse, rows, sems, *, many,
):
    elems = blocks.shape[0]
    n_side = side.shape[0] // elems
    side_copy = pltpu.make_async_copy(side_hbm, side, sems.at[elems])
    table_copy = pltpu.make_async_copy(table_hbm, table, sems.at[elems + 1])

    def block_copy(e):
        return pltpu.make_async_copy(diag_hbm.at[e], blocks.at[e], sems.at[e])

    side_copy.start()
    table_copy.start()
    for e in range(elems):
        block_copy(e).start()
    rows[...] = jnp.zeros_like(rows)
    side_copy.wait()
    table_copy.wait()
    pitch = stacked.shape[0] // NV
    face_product([(0, side)], pitch, table, stacked, products)
    for f in range(n_side):
        for v in range(NV):
            start = (2 + f) * FACE + v * UNIT
            unit = products[pl.ds(v * pitch + f, elems, stride=n_side), :]
            rows[:elems, start : start + UNIT] = unit[:, :UNIT]

    def some_blocks(step, carry):
        for i in range(many):
            block_copy(step * many + i).wait()
        for i in range(many):
            e = step * many + i
            g = coarse_block(blocks[e], right_ref[...], left_ref[...])
            coarse[pl.ds(e * NCOARSE, NCOARSE), :] = g
        return carry

    lax.fori_loop(0, elems // many, some_blocks, 0)
    for c in range(NCOARSE):
        piece = coarse[pl.ds(c, elems, stride=NCOARSE), :]
        start = DIAG_AT + c * NCOARSE
        rows[:elems, start : start + NCOARSE] = piece[:, :NCOARSE]
    out_ref[...] = rows[...].astype(BF16)


def pack_kernel(where_ref, rows_ref, minus_ref, plus_ref, owner_ref, keep_ref, send_ref, head, packed_scr, *, owners_n):
    elems = owner_ref.shape[1]
    cut = head.shape[1]
    head[...] = rows_ref[:, :cut].astype(F32)
    head[:, :FACE] = minus_ref[...].astype(F32)
    head[:, FACE : 2 * FACE] = plus_ref[...].astype(F32)
    most = keep_ref.shape[1]
    slots = owners_n * most
    placer = placement(owner_ref[...], where_ref[0], owners_n, most)
    first = jnp.dot(placer, head[:elems].astype(BF16), preferred_element_type=F32)
    rest = jnp.dot(placer, rows_ref[:elems, cut:], preferred_element_type=F32)
    for j in range(ROW_TILES):
        source, at = (first, j * LANES) if j * LANES < cut else (rest, j * LANES - cut)
        packed_scr[pl.ds(j, slots, stride=ROW_TILES), :] = source[:, at : at + LANES]
    kept = most * ROW_TILES
    keep_ref[...] = packed_scr[:kept].astype(BF16).reshape(keep_ref.shape)
    send_ref[...] = packed_scr[kept:].astype(BF16).reshape(send_ref.shape)


def unpack_kernel(where_ref, *refs, owners_n, most):
    spread_ref, out_hbm, tiles, flat, out, sems = refs[-6:]
    kept = refs[: (len(refs) - 6) // 2]
    others = refs[(len(refs) - 6) // 2 : -6]
    slots = out.shape[1]
    me = where_ref[0]
    width = NCOARSE * NCOARSE
    half = LEFT_TILES * LANES

    def copy_out(block):
        return pltpu.make_async_copy(out.at[block], out_hbm.at[block], sems.at[block])

    @pl.when(me >= owners_n)
    def _():
        for block in range(NFACES + 1):
            out[block] = jnp.zeros(out.shape[1:], BF16)
            copy_out(block).start()

    @pl.when(me < owners_n)
    def _():
        step = most * ROW_TILES
        for a in range(len(kept)):
            for j in range(owners_n):
                chunk = kept[a][0] if j == 0 else others[a][j - 1]
                source = a * owners_n + lax.rem(me - j + owners_n, owners_n)
                tiles[pl.ds(source * step, step), :] = chunk.astype(F32).reshape(step, LANES)
        for j in range(ROW_TILES):
            flat[:, j * LANES : (j + 1) * LANES] = tiles[pl.ds(j, slots, stride=ROW_TILES), :]
        out[0] = flat[:, DIAG_AT : DIAG_AT + width].astype(BF16)
        copy_out(0).start()
        for f in range(NFACES):
            sums = {}
            for parity in range(2):
                vs = list(range(parity, NV, 2))
                cuts = [f * FACE + v * UNIT for v in vs]
                units = jnp.concatenate([flat[:, c : c + UNIT] for c in cuts], axis=0).astype(BF16)
                table = spread_ref[f, :, parity * half : (parity + 1) * half]
                spread = jnp.dot(units, table, preferred_element_type=F32)
                for row, v in enumerate(vs):
                    for t in range(LEFT_TILES):
                        tile = v * VROW // LANES + t
                        if tile * LANES >= width:
                            continue
                        value = spread[row * slots : (row + 1) * slots, t * LANES : (t + 1) * LANES]
                        sums[tile] = sums[tile] + value if tile in sums else value
            for tile, value in sums.items():
                cut = min(LANES, width - tile * LANES)
                out[f + 1, :, tile * LANES : tile * LANES + cut] = value[:, :cut].astype(BF16)
            copy_out(f + 1).start()

    for block in range(NFACES + 1):
        copy_out(block).wait()


def call(kernel, out_shape, scratch, *args, **kwargs):
    return pl.pallas_call(kernel, out_shape=out_shape, scratch_shapes=scratch, **kwargs)(*args)


def shards(diag_jac, xface_jac, side_jac, orient, owner):
    elems = diag_jac.shape[0]
    nf = diag_jac.shape[1]
    length = xface_jac.shape[2]
    pad = round_up(elems, 16)
    grp_size = lax.axis_size("grp")
    slab_size = lax.axis_size("slab")
    owners_n = grp_size // GROUPS
    most = max(2, 3 * elems // (2 * owners_n))
    where = lax.axis_index("grp").astype(jnp.int32)[None]
    table = jnp.asarray(face_table())
    right, left = (jnp.asarray(t) for t in diag_tables())

    sds = jax.ShapeDtypeStruct
    width = table.shape[1]
    plus, sent = call(
        xface_kernel,
        (sds((pad, FACE), BF16), sds((pad, FACE), BF16)),
        [
            pltpu.VMEM((NV * 2 * pad, width), BF16),
            pltpu.VMEM((NV * 2 * pad, LANES), F32),
            pltpu.VMEM((pad, FACE), F32),
        ],
        jnp.transpose(xface_jac, (1, 0, 2)), table, jnp.asarray(turn_tables()), orient[None, :], name="xface",
    )
    minus = lax.ppermute(sent, "slab", [(i, (i + 1) % slab_size) for i in range(slab_size)])

    many = max(n for n in range(1, 4) if elems % n == 0)
    n_side = side_jac.shape[1]
    pitch = round_up(n_side * elems, 16)
    chunk = (most, ROW_TILES, LANES)
    rows = call(
        functools.partial(main_kernel, many=many),
        sds((pad, ROW_TILES * LANES), BF16),
        [
            pltpu.VMEM((elems, nf, nf), BF16),
            pltpu.VMEM((n_side * elems, length), BF16),
            pltpu.VMEM(table.shape, BF16),
            pltpu.VMEM((NV * pitch, width), BF16),
            pltpu.VMEM((NV * pitch, LANES), F32),
            pltpu.VMEM((elems * NCOARSE, LANES), F32),
            pltpu.VMEM((pad, ROW_TILES * LANES), F32),
            pltpu.SemaphoreType.DMA((elems + 2,)),
        ],
        diag_jac, side_jac.reshape(n_side * elems, length), table, right, left,
        in_specs=[pl.BlockSpec(memory_space=pl.ANY)] * 3 + [VMEM] * 2,
        name="main",
    )
    keep, send = call(
        functools.partial(pack_kernel, owners_n=owners_n),
        (sds((1,) + chunk, BF16), sds((owners_n - 1,) + chunk, BF16)),
        [
            pltpu.VMEM((pad, round_up(2 * FACE, LANES)), F32),
            pltpu.VMEM((owners_n * most * ROW_TILES, LANES), F32),
        ],
        where, rows, minus, plus, owner[None, :],
        in_specs=[SMALL] + [VMEM] * 4,
        name="pack",
    )

    groups = grp_size // owners_n

    def to_owners(array, a, j):
        pairs = [(a * owners_n + o, (o + j) % owners_n) for o in range(owners_n)]
        return lax.ppermute(array, "grp", pairs)

    kept = [keep] + [to_owners(keep, a, 0) for a in range(1, groups)]
    others = []
    for a in range(groups):
        pieces = [to_owners(send[j - 1 : j], a, j) for j in range(1, owners_n)]
        others.append(jnp.concatenate(pieces, axis=0) if len(pieces) > 1 else pieces[0])
    sources = kept + others

    slots = grp_size * most
    rows = call(
        functools.partial(unpack_kernel, owners_n=owners_n, most=most),
        sds((NFACES + 1, slots, NCOARSE * NCOARSE), BF16),
        [
            pltpu.VMEM((slots * ROW_TILES, LANES), F32),
            pltpu.VMEM((slots, ROW_TILES * LANES), F32),
            pltpu.VMEM((NFACES + 1, slots, NCOARSE * NCOARSE), BF16),
            pltpu.SemaphoreType.DMA((NFACES + 1,)),
        ],
        where, *sources, jnp.asarray(spread_tables()),
        in_specs=[SMALL] + [VMEM] * (len(sources) + 1),
        out_specs=pl.BlockSpec(memory_space=pl.ANY),
        name="unpack",
    )
    return jnp.transpose(rows, (1, 0, 2))


def solution(mesh):
    in_specs = (
        P(("slab", "grp"), None, None),
        P(("slab", "grp"), None, None),
        P(("slab", "grp"), None, None),
        P(("slab", "grp")),
        P(("slab", "grp")),
    )
    out_specs = P(("slab", "grp"), None, None)
    return jax.shard_map(shards, mesh=mesh, in_specs=in_specs, out_specs=out_specs, check_vma=False)
```
